128 devices in a mesh: grp: 4 (over x_lo, core), seq: 32 (over x_hi, z, y).
Axes of the slice: x: 4 (x_hi: 2, x_lo: 2; x = x_hi * 2 + x_lo), y: 4, z: 4, core: 2. Of those that a mesh axis runs over, the one named last changes fastest.
Arguments:
- patches: bfloat16 [8192, 1280], P(('grp', 'seq')), may hold values from -60 to 60
- piece_ids: int32 [128, 64], P(('grp', 'seq')), may hold values from 0 to 2, never falling along the last dimension, each value on 1 to 48 neighbouring positions
- vit_gain: float32 [1280], replicated, may hold values from 0.25 to 1.75
- vit_qkv: bfloat16 [1280, 3840], replicated
- vit_out: bfloat16 [1280, 1280], replicated, may hold values from -0.15625 to 0.15625
- merge_gain: float32 [1280], replicated, may hold values from 0.25 to 1.75
- merge_up: bfloat16 [5120, 5120], P(None, 'seq'), may hold values from -0.078125 to 0.078125
- merge_down: bfloat16 [5120, 8192], P(None, 'seq'), may hold values from -0.078125 to 0.078125
- dest: int32 [2048], P(('grp', 'seq')), may hold values from 0 to 31, as said below
- tokens: bfloat16 [32768, 8192], P(('grp', 'seq')), may hold values from -60 to 60
- image_index: int32 [32768], P(('grp', 'seq')), may hold values from 0 to 32, as said below
- doc_lengths: int32 [4, 4], P('grp'), may hold values from 1 to 4096, 8192 in all within a row
- attn_gain: float32 [8192], replicated, may hold values from 0.25 to 1.75
- attn_qkv: bfloat16 [8192, 768], P(('grp', 'seq'))
- attn_out: bfloat16 [512, 8192], P(None, ('grp', 'seq')), may hold values from -0.25 to 0.25
Outputs:
- layer_out: bfloat16 [32768, 8192], P(('grp', 'seq'))
The draws below stay inside these ranges and needn't reach their ends.
Inputs may be any that keep to these rules, and one draw needn't show every extreme that they name: `dest`: within each aligned block of 16 rows (one device's merged rows), exactly 16 distinct values occur, each exactly 1 times, and in every group one device is named by every device of the group. `image_index`: 32 marks a text token. A value k < 32 on a device names the merged row that the device of seq index k // 1 in its group sends to it as its (k % 1)-th row in row order; each such row is named by exactly one token of the receiving device, and no other values occur. `piece_ids`: piece numbers never fall within a window. `doc_lengths`: each group's documents fill its 8192 positions.
All inputs are finite; a program needn't handle non-finite values.
Results may differ from the reference program's by a relative error of at most 0.0093.
The reference program's roundings to bfloat16 on the way count: a program that leaves them out, or rounds other values in their place, can miss the bound.
Values may be sent and summed in bfloat16 or wider, within the bound.
No kernel may reach another device: no remote copies, remote signals or barrier semaphores. Data moves between devices by JAX's collectives and lax.ppermute only.
A program may use at most 192 MiB of HBM per device.

```python
import math
import jax
import jax.numpy as jnp
import numpy as np
from jax import lax

D = 8192
VD = 1280
VHEADS = 16
HEAD = 128
HQ = 4
WIN = 64
DOCS = 4
TOK_DEV = 256
M_DEV = 16
CAP = 1
SLOTS = 32
PATCHES = 8192
WINDOWS = 128
MERGED = 2048
GROUP_TOK = 8192
TOKENS = 32768
MOST_DOC = 4096
N_GRP = 4
N_SEQ = 32


def scaled_field(key, row_count, col_count):
    parts = jax.random.split(key, 3)
    row_scale = jnp.exp(jax.random.uniform(parts[1], (row_count, 1), jnp.float32, jnp.log(0.3), jnp.log(3.0)))
    col_scale = jnp.exp(jax.random.uniform(parts[2], (1, col_count), jnp.float32, jnp.log(0.3), jnp.log(3.0)))
    base = jnp.clip(jax.random.normal(parts[0], (row_count, col_count), jnp.float32), -6.0, 6.0)
    return base * row_scale * col_scale


def draw_patches(key, part):
    return scaled_field(jax.random.fold_in(key, 11), PATCHES, VD).astype(jnp.bfloat16)


def draw_tokens(key, part):
    return scaled_field(jax.random.fold_in(key, 12), TOKENS, D).astype(jnp.bfloat16)


def draw_vit_qkv(key, part):
    parts = jax.random.split(jax.random.fold_in(key, 13), 1)
    base = jnp.clip(jax.random.normal(parts[0], (VD, 3 * VD), jnp.float32), -6.0, 6.0) * VD ** (-0.5)
    return base.astype(jnp.bfloat16)


def draw_attn_qkv(key, part):
    parts = jax.random.split(jax.random.fold_in(key, 14), 1)
    base = jnp.clip(jax.random.normal(parts[0], (D, (HQ + 2) * HEAD), jnp.float32), -6.0, 6.0) * D ** (-0.5)
    return base.astype(jnp.bfloat16)


def route_tables(key):
    base_key = jax.random.fold_in(key, 5)
    fanout = N_SEQ // 2
    sequence_ids = jnp.arange(N_SEQ, dtype=jnp.int32)
    row_ids = jnp.arange(M_DEV, dtype=jnp.int32)
    slot_ids = jnp.arange(CAP, dtype=jnp.int32)

    def one_group(group_key):
        parts = jax.random.split(group_key, 4)
        preference_boost = jax.random.permutation(parts[0], N_SEQ).astype(jnp.int32)
        random_jitter = jax.random.randint(parts[1], (N_SEQ, N_SEQ), 0, 1 << 20, dtype=jnp.int32)
        extra_reward = jnp.where(preference_boost == 0, 1 << 22, (N_SEQ - preference_boost) * (1 << 14)).astype(jnp.int32)
        score_value = (random_jitter + extra_reward[None, :]) * N_SEQ + sequence_ids[None, :]
        chosen = lax.top_k(score_value, fanout)[1].astype(jnp.int32)
        shuffles = jax.vmap(lambda shuffle_key: jax.random.permutation(shuffle_key, M_DEV))(jax.random.split(parts[2], N_SEQ)).astype(jnp.int32)
        targets = jnp.take_along_axis(chosen, shuffles // CAP, axis=1)
        same = targets[:, :, None] == targets[:, None, :]
        earlier = row_ids[None, :] < row_ids[:, None]
        order = jnp.sum(same & earlier[None], axis=-1).astype(jnp.int32)
        match = (targets[None, :, None, :] == sequence_ids[:, None, None, None]) & (order[None, :, None, :] == slot_ids[None, None, :, None])
        filled = jnp.any(match, axis=-1).reshape(N_SEQ, SLOTS)
        places = jax.vmap(lambda place_key: jax.random.permutation(place_key, TOK_DEV)[:SLOTS])(jax.random.split(parts[3], N_SEQ)).astype(jnp.int32)
        token_ids = jnp.arange(TOK_DEV, dtype=jnp.int32)
        hit = (places[:, :, None] == token_ids[None, None, :]) & filled[:, :, None]
        slot_all = jnp.arange(SLOTS, dtype=jnp.int32)
        named = jnp.sum(jnp.where(hit, slot_all[None, :, None], 0), axis=1)
        index = named + jnp.where(jnp.any(hit, axis=1), 0, SLOTS)
        return (targets.reshape(-1), index.reshape(-1))
    targets_all, index_all = jax.vmap(one_group)(jax.random.split(base_key, N_GRP))
    return (targets_all.reshape(-1).astype(jnp.int32), index_all.reshape(-1).astype(jnp.int32))


def draw_dest(key, part):
    return route_tables(key)[0]


def draw_image_index(key, part):
    return route_tables(key)[1]


def block_scale(own_key, shape, pieces, low, top_value):
    loudness, own = 1.0, jax.random.fold_in(own_key, 6)
    for position, blocks in pieces:
        steps = jnp.exp(jax.random.uniform(jax.random.fold_in(own, position), (blocks,), jnp.float32, low / len(pieces), top_value / len(pieces)))
        loudness = loudness * jnp.repeat(steps, shape[position] // blocks).reshape([-1 if axis == position else 1 for axis in range(len(shape))])
    return loudness


def length_profile(count, total, bound, skew):
    weights = [(1 << 20) // math.isqrt(standing ** skew) + 1 for standing in range(2, count + 1)]
    surplus, holding = total - bound - (count - 1), [1] * (count - 1)
    while surplus > 0:
        candidates = [i for i in range(count - 1) if holding[i] < bound]
        pool, budget = sum([weights[i] for i in candidates]), surplus
        for i in candidates:
            addition = min(bound - holding[i], max(1, budget * weights[i] // pool), surplus)
            holding[i] = holding[i] + addition
            surplus = surplus - addition
    return np.array([bound] + holding)


def ragged_sizes(key, number_of, total, limit, lean):
    if number_of == 2:
        one = jax.random.randint(key, (), max(1, total - limit), min(limit, total - 1) + 1)
        return jnp.stack([one, total - one])
    sizes = jnp.asarray(length_profile(number_of, total, limit, lean), jnp.int32)
    couples = (number_of - 1) // 2
    giver, taker = sizes[1:1 + 2 * couples:2], sizes[2:2 + 2 * couples:2]
    room = jnp.minimum(giver - 1, limit - taker)
    shifted = jax.random.randint(jax.random.fold_in(key, 1), (couples,), 0, 1 << 20) % (room + 1)
    sizes = sizes.at[1:1 + 2 * couples:2].set(giver - shifted).at[2:2 + 2 * couples:2].set(taker + shifted)
    return sizes[jax.random.permutation(jax.random.fold_in(key, 2), number_of)]


def centred(own_key, shape, width, reach, cuts=(), held_as=jnp.bfloat16):
    level = block_scale(own_key, shape, cuts, -0.22, 0.18) if cuts else 1.0
    result = jax.random.normal(own_key, shape, jnp.float32) * width * level
    return jnp.minimum(jnp.maximum(result, -reach), reach).astype(held_as)


def setup_inputs(seed: int = 0) -> dict:
    key_list = jax.random.split(jax.random.key(seed), 16)
    patches = draw_patches(jax.random.fold_in(key_list[15], 71), 0)
    piece_ids = jax.vmap(lambda own: jnp.searchsorted(jnp.cumsum(ragged_sizes(own, 3, WIN, 48, 2)), jnp.arange(WIN), side="right"))(jax.random.split(key_list[1], WINDOWS)).reshape((WINDOWS, WIN)).astype(jnp.int32)
    vit_gain = jnp.clip(1.0 + 0.15 * jax.random.normal(key_list[2], (VD,), jnp.float32), 0.25, 1.75)
    vit_qkv = draw_vit_qkv(jax.random.fold_in(key_list[15], 71), 0)
    vit_out = centred(key_list[4], (VD, VD), VD ** -0.5, 0.15625)
    merge_gain = jnp.clip(1.0 + 0.15 * jax.random.normal(key_list[5], (VD,), jnp.float32), 0.25, 1.75)
    merge_up = centred(key_list[6], (4 * VD, 4 * VD), (4 * VD) ** -0.5, 0.078125, ((1, 32),))
    merge_down = centred(key_list[7], (4 * VD, D), (4 * VD) ** -0.5, 0.078125, ((1, 32),))
    dest = draw_dest(jax.random.fold_in(key_list[15], 71), 0)
    tokens = draw_tokens(jax.random.fold_in(key_list[15], 71), 0)
    image_index = draw_image_index(jax.random.fold_in(key_list[15], 71), 0)
    doc_lengths = jax.vmap(lambda own: ragged_sizes(own, DOCS, GROUP_TOK, MOST_DOC, 2))(jax.random.split(key_list[11], N_GRP)).reshape((N_GRP, DOCS)).astype(jnp.int32)
    attn_gain = jnp.clip(1.0 + 0.15 * jax.random.normal(key_list[12], (D,), jnp.float32), 0.25, 1.75)
    attn_qkv = draw_attn_qkv(jax.random.fold_in(key_list[15], 71), 0)
    attn_out = centred(key_list[14], (HQ * HEAD, D), (HQ * HEAD) ** -0.5, 0.25, ((1, 128),))
    return dict(patches=patches, piece_ids=piece_ids, vit_gain=vit_gain, vit_qkv=vit_qkv, vit_out=vit_out, merge_gain=merge_gain, merge_up=merge_up, merge_down=merge_down, dest=dest, tokens=tokens, image_index=image_index, doc_lengths=doc_lengths, attn_gain=attn_gain, attn_qkv=attn_qkv, attn_out=attn_out)


EPSILON = 1e-06

def rms_scale(inputs, gain):
    mean_square = lax.optimization_barrier(jnp.mean(inputs * inputs, axis=-1, keepdims=True))
    return inputs * lax.rsqrt(mean_square + EPSILON) * gain

def softmax_mix(scores, allowed, value_collection, spec):
    scores = jnp.where(allowed[None], scores, -1e+30)
    highest = lax.optimization_barrier(jnp.max(scores, axis=-1, keepdims=True))
    weights = jnp.exp(scores - highest)
    totals = lax.optimization_barrier(jnp.sum(weights, axis=-1))
    rounded_values = lax.optimization_barrier(weights.astype(jnp.bfloat16)).astype(jnp.float32)
    mixture = jnp.einsum(spec, rounded_values, value_collection.astype(jnp.float32))
    return mixture / jnp.transpose(totals)[:, :, None]

def window_layer(patch_rows, piece_rows, vit_gain, vit_qkv, vit_out, merge_gain):
    row_count, features = patch_rows.shape
    head_dim = features // VHEADS
    residual = patch_rows.astype(jnp.float32)
    normed = rms_scale(residual, vit_gain).astype(jnp.bfloat16)
    projected = jnp.dot(normed, vit_qkv, preferred_element_type=jnp.float32).astype(jnp.bfloat16)
    queries = projected[:, :features].reshape(row_count, VHEADS, head_dim)
    key_set = projected[:, features:2 * features].reshape(row_count, VHEADS, head_dim)
    value_collection = projected[:, 2 * features:].reshape(row_count, VHEADS, head_dim)
    scores = jnp.einsum('qhd,khd->hqk', queries.astype(jnp.float32), key_set.astype(jnp.float32)) * head_dim ** (-0.5)
    frames = jnp.arange(row_count, dtype=jnp.int32) // WIN
    allowed = (frames[:, None] == frames[None, :]) & (piece_rows[:, None] == piece_rows[None, :])
    mixture = softmax_mix(scores, allowed, value_collection, 'hqk,khd->qhd')
    mixture = mixture.reshape(row_count, features).astype(jnp.bfloat16)
    residual = residual + jnp.dot(mixture, vit_out, preferred_element_type=jnp.float32)
    merge_input = rms_scale(residual, merge_gain).astype(jnp.bfloat16)
    return merge_input.reshape(row_count // 4, 4 * features)

def attend(query_rows, query_pos, query_start, key_value, key_pos):
    row_count = query_rows.shape[0]
    head_dim = key_value.shape[1] // 2
    heads = query_rows.shape[1] // head_dim
    queries = query_rows.reshape(row_count, heads, head_dim)
    scores = jnp.einsum('qhd,kd->hqk', queries.astype(jnp.float32), key_value[:, :head_dim].astype(jnp.float32)) * head_dim ** (-0.5)
    allowed = (key_pos[None, :] >= query_start[:, None]) & (key_pos[None, :] <= query_pos[:, None])
    mixture = softmax_mix(scores, allowed, key_value[:, head_dim:], 'hqk,kd->qhd')
    return mixture.reshape(row_count, heads * head_dim).astype(jnp.bfloat16)

def slot_numbers(targets):
    row_count = targets.shape[-1]
    order = jnp.arange(row_count, dtype=jnp.int32)
    same = targets[..., :, None] == targets[..., None, :]
    earlier = order[None, :] < order[:, None]
    return lax.optimization_barrier(jnp.sum(same & earlier, axis=-1)).astype(jnp.int32)

def prefill_group(layer_in, lengths, attn_gain, attn_qkv, attn_out):
    normed = rms_scale(layer_in.astype(jnp.float32), attn_gain).astype(jnp.bfloat16)
    projected = jnp.dot(normed, attn_qkv, preferred_element_type=jnp.float32).astype(jnp.bfloat16)
    query_width = HQ * HEAD
    queries = projected[:, :query_width]
    key_value = projected[:, query_width:]
    positions = jnp.arange(GROUP_TOK, dtype=jnp.int32)
    starts = (jnp.cumsum(lengths) - lengths).astype(jnp.int32)
    doc_start = lax.optimization_barrier(jnp.max(jnp.where(starts[None, :] <= positions[:, None], starts[None, :], 0), axis=1)).astype(jnp.int32)
    block_rows = min(GROUP_TOK, 512)
    attended = lax.map(lambda parts: attend(parts[0], parts[1], parts[2], key_value, positions), (queries.reshape(-1, block_rows, query_width), positions.reshape(-1, block_rows), doc_start.reshape(-1, block_rows))).reshape(GROUP_TOK, query_width)
    update = jnp.dot(attended, attn_out, preferred_element_type=jnp.float32)
    return (layer_in.astype(jnp.float32) + update).astype(jnp.bfloat16)

def reference(patches, piece_ids, vit_gain, vit_qkv, vit_out, merge_gain, merge_up, merge_down, dest, tokens, image_index, doc_lengths, attn_gain, attn_qkv, attn_out):
    block_len = WIN
    patch_blocks = patches.reshape(PATCHES // block_len, block_len, VD)
    piece_blocks = piece_ids.reshape(PATCHES // block_len, block_len)
    merge_input = lax.map(lambda parts: window_layer(parts[0], parts[1], vit_gain, vit_qkv, vit_out, merge_gain), (patch_blocks, piece_blocks)).reshape(MERGED, 4 * VD)
    hidden = jax.nn.gelu(jnp.dot(merge_input, merge_up, preferred_element_type=jnp.float32), approximate=False).astype(jnp.bfloat16)
    merged_rows = jnp.dot(hidden, merge_down, preferred_element_type=jnp.float32).astype(jnp.bfloat16)
    merged_rows = merged_rows.reshape(N_GRP, N_SEQ, M_DEV, D)
    targets = dest.reshape(N_GRP, N_SEQ, M_DEV)
    orders = slot_numbers(targets)
    receivers = jnp.arange(N_SEQ, dtype=jnp.int32)
    row_ids = jnp.arange(M_DEV, dtype=jnp.int32)
    slot_ids = jnp.arange(CAP, dtype=jnp.int32)
    index_all = image_index.reshape(N_GRP, N_SEQ, TOK_DEV)
    token_all = tokens.reshape(N_GRP, N_SEQ, TOK_DEV, D)
    results = []
    for group in range(N_GRP):
        match = (targets[group][None, :, None, :] == receivers[:, None, None, None]) & (orders[group][None, :, None, :] == slot_ids[None, None, :, None])
        row_pick = lax.optimization_barrier(jnp.sum(jnp.where(match, row_ids, 0), axis=-1)).astype(jnp.int32)
        source_list = jnp.broadcast_to(receivers[None, :, None], row_pick.shape)
        table = merged_rows[group][source_list, row_pick].reshape(N_SEQ, SLOTS, D)
        index_rows = index_all[group]
        picked = jax.vmap(lambda table_rows, wanted: table_rows[jnp.minimum(wanted, SLOTS - 1)])(table, index_rows)
        layer_in = jnp.where((index_rows < SLOTS)[:, :, None], picked, token_all[group]).reshape(GROUP_TOK, D)
        results.append(prefill_group(layer_in, doc_lengths[group], attn_gain, attn_qkv, attn_out))
    return jnp.concatenate(results, axis=0)
```

```python
import jax
import jax.numpy as jnp
from jax import lax
from jax.sharding import Mesh
from jax.sharding import PartitionSpec as P

VHEADS = 16
WIN = 64
SEQ = ("seq_0", "seq_1", "seq_2")
GRP_SEQ = ("grp_0", "grp_1", "seq_0", "seq_1", "seq_2")
GRP = ("grp_0", "grp_1")


EPSILON = 1e-06


def cut_rows(length, count):
    lap = length // count
    if lap >= 8:
        lap -= lap % 8
    return [lap * k for k in range(1, count)]


def all_blocks(x, axes, turns):
    parts = x[None]
    for k in turns:
        parts = lax.all_gather(parts, axes[k], axis=0, tiled=True)
    current = [lax.axis_size(axes[k]) for k in reversed(turns)]
    parts = parts.reshape(*current, *x.shape)
    turned = sorted(range(len(turns)), key=lambda place: turns[len(turns) - 1 - place])
    return parts.transpose(*turned, *range(len(turns), parts.ndim)).reshape(-1, *x.shape)


def joined_along(parts, dim):
    parts = jnp.moveaxis(parts, 0, dim)
    shape = parts.shape
    return parts.reshape(*shape[:dim], shape[dim] * shape[dim + 1], *shape[dim + 2 :])


def gather_all_axes(x, axes, dim):
    widest = max(range(max(1, x.ndim - 1)), key=lambda d: x.shape[d])
    count, outs = (len(axes), [])
    for first, slab in enumerate(jnp.split(x, cut_rows(x.shape[widest], count), axis=widest)):
        if slab.size:
            turns = [(first - k) % count for k in range(count)]
            outs.append(all_blocks(slab, axes, turns))
    return joined_along(jnp.concatenate(outs, axis=widest + 1), dim)


def from_behind(value, axis, steps):
    count = lax.axis_size(axis)
    first, last = (max(0, -steps), min(count, count - steps))
    return lax.ppermute(value, axis, [(source, source + steps) for source in range(first, last)])


def rms_scale(inputs, gain):
    mean_square = jnp.mean(inputs * inputs, axis=-1, keepdims=True)
    return inputs * lax.rsqrt(mean_square + EPSILON) * gain


def softmax_mix(scores, allowed, value_collection, spec):
    scores = jnp.where(allowed[None], scores, -1e30)
    highest = jnp.max(scores, axis=-1, keepdims=True)
    weights = jnp.exp(scores - highest)
    totals = jnp.sum(weights, axis=-1)
    mixture = jnp.einsum(
        spec, weights.astype(jnp.bfloat16), value_collection, preferred_element_type=jnp.float32
    )
    return mixture / jnp.transpose(totals)[:, :, None]


def window_layer(patch_rows, piece_rows, vit_gain, vit_qkv, vit_out, merge_gain):
    row_count, features = patch_rows.shape
    head_dim = features // VHEADS
    residual = patch_rows.astype(jnp.float32)
    normed = rms_scale(residual, vit_gain).astype(jnp.bfloat16)
    projected = jnp.dot(normed, vit_qkv, preferred_element_type=jnp.float32).astype(jnp.bfloat16)
    queries = projected[:, :features].reshape(row_count, VHEADS, head_dim)
    key_set = projected[:, features : 2 * features].reshape(row_count, VHEADS, head_dim)
    value_collection = projected[:, 2 * features :].reshape(row_count, VHEADS, head_dim)
    scores = jnp.einsum(
        "qhd,khd->hqk", queries, key_set, preferred_element_type=jnp.float32
    ) * head_dim ** (-0.5)
    frames = jnp.arange(row_count, dtype=jnp.int32) // WIN
    allowed = (frames[:, None] == frames[None, :]) & (piece_rows[:, None] == piece_rows[None, :])
    mixture = softmax_mix(scores, allowed, value_collection, "hqk,khd->qhd")
    mixture = mixture.reshape(row_count, features).astype(jnp.bfloat16)
    residual = residual + jnp.dot(mixture, vit_out, preferred_element_type=jnp.float32)
    merge_input = rms_scale(residual, merge_gain).astype(jnp.bfloat16)
    return merge_input.reshape(row_count // 4, 4 * features)


def attend(query_rows, query_pos, query_start, key_value, key_pos):
    row_count = query_rows.shape[0]
    head_dim = key_value.shape[1] // 2
    heads = query_rows.shape[1] // head_dim
    queries = query_rows.reshape(row_count, heads, head_dim)
    scores = jnp.einsum(
        "qhd,kd->hqk", queries, key_value[:, :head_dim], preferred_element_type=jnp.float32
    ) * head_dim ** (-0.5)
    allowed = (key_pos[None, :] >= query_start[:, None]) & (key_pos[None, :] <= query_pos[:, None])
    mixture = softmax_mix(scores, allowed, key_value[:, head_dim:], "hqk,kd->qhd")
    return mixture.reshape(row_count, heads * head_dim).astype(jnp.bfloat16)


def slot_numbers(targets):
    row_count = targets.shape[-1]
    order = jnp.arange(row_count, dtype=jnp.int32)
    same = targets[..., :, None] == targets[..., None, :]
    earlier = order[None, :] < order[:, None]
    return jnp.sum(same & earlier, axis=-1)


def on_device(
    patches,
    piece_ids,
    vit_gain,
    vit_qkv,
    vit_out,
    merge_gain,
    merge_up,
    merge_down,
    dest,
    tokens,
    image_index,
    doc_lengths,
    attn_gain,
    attn_qkv,
    attn_out,
):
    features = patches.shape[1]
    block_len = WIN
    patch_blocks = patches.reshape(-1, block_len, features)
    merge_input = lax.map(
        lambda parts: window_layer(parts[0], parts[1], vit_gain, vit_qkv, vit_out, merge_gain),
        (patch_blocks, piece_ids),
    ).reshape(-1, 4 * features)
    own_rows = merge_input.shape[0]
    seq_count = lax.axis_size(SEQ)
    seq_index = lax.axis_index(SEQ)
    hidden_part = jax.nn.gelu(
        jnp.dot(
            lax.all_gather(merge_input, SEQ, axis=0, tiled=True),
            merge_up,
            preferred_element_type=jnp.float32,
        ),
        approximate=False,
    ).astype(jnp.bfloat16)
    column_part = jnp.dot(
        lax.all_gather(hidden_part, SEQ, axis=1, tiled=True),
        merge_down,
        preferred_element_type=jnp.float32,
    ).astype(jnp.bfloat16)
    capacity = own_rows // (seq_count // 2)
    slots = seq_count * capacity
    receivers = jnp.arange(seq_count, dtype=jnp.int32)
    slot_ids = jnp.arange(capacity, dtype=jnp.int32)
    home_rows = lax.all_to_all(column_part, SEQ, split_axis=0, concat_axis=1, tiled=True)
    order = slot_numbers(dest)
    select = (dest[None, None, :] == receivers[:, None, None]) & (
        order[None, None, :] == slot_ids[None, :, None]
    )
    outgoing = jnp.einsum(
        "dcj,jf->dcf", select.astype(jnp.bfloat16), home_rows, preferred_element_type=jnp.float32
    ).astype(jnp.bfloat16)
    arrived = lax.all_to_all(outgoing, SEQ, split_axis=0, concat_axis=0, tiled=True).reshape(
        slots, -1
    )
    slot_all = jnp.arange(slots, dtype=jnp.int32)
    picker = (image_index[:, None] == slot_all[None, :]).astype(jnp.bfloat16)
    pictured = jnp.dot(picker, arrived, preferred_element_type=jnp.float32).astype(jnp.bfloat16)
    layer_in = jnp.where((image_index < slots)[:, None], pictured, tokens)
    tok_rows = tokens.shape[0]
    normed = rms_scale(layer_in.astype(jnp.float32), attn_gain).astype(jnp.bfloat16)
    projected = jnp.dot(
        normed, gather_all_axes(attn_qkv, GRP_SEQ, 0), preferred_element_type=jnp.float32
    ).astype(jnp.bfloat16)
    query_width = attn_out.shape[0]
    queries = projected[:, :query_width]
    key_value = projected[:, query_width:]
    head_dim = key_value.shape[1] // 2
    head_count = query_width // head_dim
    positions = seq_index * tok_rows + jnp.arange(tok_rows, dtype=jnp.int32)
    lengths = doc_lengths[0]
    order_of = jnp.arange(lengths.shape[0], dtype=jnp.int32)
    starts = jnp.sum(jnp.where(order_of[None, :] < order_of[:, None], lengths[None, :], 0), axis=1)
    doc_start = jnp.max(
        jnp.where(starts[None, :] <= positions[:, None], starts[None, :], 0), axis=1
    )
    reach = seq_count // 2
    buffer = jnp.zeros(((reach + 1) * tok_rows, key_value.shape[1]), key_value.dtype)
    buffer = lax.dynamic_update_slice_in_dim(buffer, key_value, reach * tok_rows, 0)

    def step_back(turn, state):
        current, filled = state
        current = from_behind(current, SEQ, 1)
        filled = lax.dynamic_update_slice_in_dim(filled, current, (reach - turn) * tok_rows, 0)
        return (current, filled)

    key_rows = lax.fori_loop(1, reach + 1, step_back, (key_value, buffer))[1]
    key_pos = (seq_index - reach) * tok_rows + jnp.arange(key_rows.shape[0], dtype=jnp.int32)
    block_rows = min(tok_rows, 512)
    head_queries = queries.reshape(tok_rows, head_count, head_dim).transpose(1, 0, 2)

    def one_head(head_rows):
        return lax.map(
            lambda parts: attend(parts[0], parts[1], parts[2], key_rows, key_pos),
            (
                head_rows.reshape(-1, block_rows, head_dim),
                positions.reshape(-1, block_rows),
                doc_start.reshape(-1, block_rows),
            ),
        ).reshape(tok_rows, head_dim)

    attended = lax.map(one_head, head_queries).transpose(1, 0, 2).reshape(tok_rows, query_width)
    update = jnp.dot(
        attended,
        lax.all_gather(attn_out, GRP_SEQ, axis=1, tiled=True),
        preferred_element_type=jnp.float32,
    )
    return (layer_in.astype(jnp.float32) + update).astype(jnp.bfloat16)


def solution(mesh):
    torus = Mesh(mesh.devices.reshape(2, 2, 2, 4, 4), ("grp_0", "grp_1", "seq_0", "seq_1", "seq_2"))
    return jax.shard_map(
        on_device,
        mesh=torus,
        in_specs=(
            P(GRP_SEQ, None),
            P(GRP_SEQ, None),
            P(),
            P(),
            P(),
            P(),
            P(None, SEQ),
            P(None, SEQ),
            P(GRP_SEQ),
            P(GRP_SEQ, None),
            P(GRP_SEQ),
            P(GRP, None),
            P(),
            P(GRP_SEQ, None),
            P(None, GRP_SEQ),
        ),
        out_specs=P(GRP_SEQ, None),
        check_vma=False,
    )
```

```python
import jax
import jax.numpy as jnp
from jax import lax
from jax.experimental import pallas as pl
from jax.experimental.pallas import tpu as pltpu
from jax.sharding import Mesh
from jax.sharding import PartitionSpec as P

VHEADS = 16
XLO, CORE, XHI, Z, Y = ("grp_0", "grp_1", "seq_0", "seq_1", "seq_2")
SEQ = (XHI, Z, Y)
ZY = (Z, Y)
SAME_CORE = (XLO, XHI, Z, Y)
GRP_SEQ = (XLO, CORE, XHI, Z, Y)
GRP = (XLO, CORE)
EPSILON = 1e-06
NEG = -1e30
FAR = 1 << 30
BF = jnp.bfloat16
F32 = jnp.float32
MEM = 56 * 1024 * 1024


def dot_f32(a, b, ca=1, cb=0):
    return lax.dot_general(a, b, (((ca,), (cb,)), ((), ())), preferred_element_type=F32)


def window_kernel(x_ref, prow_ref, pcol_ref, gain_ref, w_ref, wo_ref, mgain_ref, o_ref, n_ref, p_ref):
    step = pl.program_id(0)
    rows, feats = x_ref.shape
    head = feats // VHEADS

    @pl.when(step == 0)
    def _():
        x = x_ref[...].astype(F32)
        mean = jnp.mean(x * x, axis=-1, keepdims=True)
        n_ref[...] = (x * lax.rsqrt(mean + EPSILON) * gain_ref[...]).astype(BF)

    for part in range(3):

        @pl.when(step == part)
        def _(part=part):
            p_ref[part] = dot_f32(n_ref[...], w_ref[...]).astype(BF)

    @pl.when(step == 2)
    def _():
        q, k, v = (p_ref[0], p_ref[1], p_ref[2])
        lane = lax.broadcasted_iota(jnp.int32, (rows, feats), 1)
        same = pcol_ref[...] == prow_ref[...]
        mixed = jnp.zeros((rows, feats), F32)
        for h in range(VHEADS):
            mine = (lane >= h * head) & (lane < (h + 1) * head)
            s = dot_f32(jnp.where(mine, q, jnp.zeros_like(q)), k, 1, 1) * head ** (-0.5)
            s = jnp.where(same, s, NEG)
            w = jnp.exp(s - jnp.max(s, axis=-1, keepdims=True))
            total = jnp.sum(w, axis=-1, keepdims=True)
            mixed = jnp.where(mine, dot_f32(w.astype(BF), v) / total, mixed)
        resid = x_ref[...].astype(F32) + dot_f32(mixed.astype(BF), wo_ref[...])
        mean = jnp.mean(resid * resid, axis=-1, keepdims=True)
        merged = (resid * lax.rsqrt(mean + EPSILON) * mgain_ref[...]).astype(BF)
        r_out = lax.broadcasted_iota(jnp.int32, (rows // 4, rows), 0)
        r_in = lax.broadcasted_iota(jnp.int32, (rows // 4, rows), 1)
        for j in range(4):
            pick = jnp.where(r_in == 4 * r_out + j, 1.0, 0.0).astype(BF)
            o_ref[:, j * feats : (j + 1) * feats] = dot_f32(pick, merged).astype(BF)


def window_layer(patches, piece_ids, vit_gain, vit_qkv, vit_out, merge_gain):
    rows, feats = patches.shape
    whole = lambda *shape: pl.BlockSpec(shape, lambda i: (0,) * len(shape))
    return pl.pallas_call(
        window_kernel,
        grid=(3,),
        in_specs=[
            whole(rows, feats),
            whole(1, rows),
            whole(rows, 1),
            whole(1, feats),
            pl.BlockSpec((feats, feats), lambda i: (0, i)),
            whole(feats, feats),
            whole(1, feats),
        ],
        out_specs=whole(rows // 4, 4 * feats),
        out_shape=jax.ShapeDtypeStruct((rows // 4, 4 * feats), BF),
        scratch_shapes=[pltpu.VMEM((rows, feats), BF), pltpu.VMEM((3, rows, feats), BF)],
        compiler_params=pltpu.CompilerParams(vmem_limit_bytes=MEM),
        name="window_layer",
    )(
        patches,
        piece_ids.reshape(1, rows),
        piece_ids.reshape(rows, 1),
        vit_gain.reshape(1, feats),
        vit_qkv,
        vit_out,
        merge_gain.reshape(1, feats),
    )


def project_kernel(core_ref, x_ref, gain_ref, own_ref, oth_ref, o_ref, r_ref, acc_ref):
    step = pl.program_id(0)
    depth = own_ref.shape[1]
    core = core_ref[0]

    @pl.when(step == 0)
    def _():
        rows, width = x_ref.shape
        total = jnp.zeros((rows, 1), F32)
        for c in range(0, width, 1024):
            x = x_ref[:, c : c + 1024].astype(F32)
            total = total + jnp.sum(x * x, axis=-1, keepdims=True)
        r_ref[...] = lax.rsqrt(total / width + EPSILON)
        acc_ref[...] = jnp.zeros_like(acc_ref)

    def add(w_ref, which):
        start = pl.multiple_of(((step % 2) * 2 + which) * depth, depth)
        x = x_ref[:, pl.ds(start, depth)].astype(F32)
        n = (x * r_ref[...] * gain_ref[:, pl.ds(start, depth)]).astype(BF)
        acc_ref[...] += dot_f32(n, w_ref[0])

    @pl.when(step < 2)
    def _():
        add(own_ref, core)

    @pl.when(step >= 2)
    def _():
        add(oth_ref, 1 - core)

    @pl.when(step == 3)
    def _():
        o_ref[...] = acc_ref[...].astype(BF)


def project(core, x, gain, own, oth):
    rows, width = x.shape
    depth, cols = own.shape[1:]
    return pl.pallas_call(
        project_kernel,
        grid_spec=pltpu.PrefetchScalarGridSpec(
            num_scalar_prefetch=1,
            grid=(4,),
            in_specs=[
                pl.BlockSpec((rows, width), lambda i, c: (0, 0)),
                pl.BlockSpec((1, width), lambda i, c: (0, 0)),
                pl.BlockSpec((1, depth, cols), lambda i, c: (jnp.minimum(i, 1), 0, 0)),
                pl.BlockSpec((1, depth, cols), lambda i, c: (jnp.maximum(i - 2, 0), 0, 0)),
            ],
            out_specs=pl.BlockSpec((rows, cols), lambda i, c: (0, 0)),
            scratch_shapes=[pltpu.VMEM((rows, 1), F32), pltpu.VMEM((rows, cols), F32)],
        ),
        out_shape=jax.ShapeDtypeStruct((rows, cols), BF),
        compiler_params=pltpu.CompilerParams(vmem_limit_bytes=MEM),
        name="project",
    )(core, x, gain.reshape(1, width), own, oth)


def attention_kernel(
    own_ref, img_ref, kv_ref, kvi_ref, index_ref, qpos_ref, qstart_ref, kpos_ref, ownpos_ref, ipos_ref, iown_ref,
    o_ref, m_ref, l_ref, acc_ref,
):
    rows = own_ref.shape[0]
    slots = img_ref.shape[0]
    head = kv_ref.shape[2] // 2
    heads = o_ref.shape[1] // head
    width = heads * head
    blocks = kv_ref.shape[0]
    m_ref[...] = jnp.full_like(m_ref, NEG)
    l_ref[...] = jnp.zeros_like(l_ref)
    acc_ref[...] = jnp.zeros_like(acc_ref)
    index = index_ref[...]
    picker = (index == lax.broadcasted_iota(jnp.int32, (rows, slots), 1)).astype(F32).astype(BF)
    is_img = index < slots
    queries = [
        jnp.where(
            is_img,
            dot_f32(picker, img_ref[:, h * head : (h + 1) * head]),
            own_ref[:, h * head : (h + 1) * head].astype(F32),
        ).astype(BF)
        for h in range(heads)
    ]
    qpos, qstart = (qpos_ref[...], qstart_ref[...])
    scale = head ** (-0.5)

    def fold(keys, values, kpos):
        allowed = (kpos >= qstart) & (kpos <= qpos)
        for h in range(heads):
            s = jnp.where(allowed, dot_f32(queries[h], keys, 1, 1) * scale, NEG)
            old = m_ref[h]
            new = jnp.maximum(old, jnp.max(s, axis=-1, keepdims=True))
            shrink = jnp.exp(old - new)
            w = jnp.exp(s - new)
            l_ref[h] = l_ref[h] * shrink + jnp.sum(w, axis=-1, keepdims=True)
            acc_ref[h] = acc_ref[h] * shrink + dot_f32(w.astype(BF), values)
            m_ref[h] = new

    fold(own_ref[:, width : width + head], own_ref[:, width + head :], ownpos_ref[...])
    fold(img_ref[:, width : width + head], img_ref[:, width + head :], iown_ref[...])
    fold(kvi_ref[:, :head], kvi_ref[:, head:], ipos_ref[...])

    def step(i, carry):
        pair = kv_ref[pl.ds(2 * i, 2), :rows, :].reshape(2 * rows, 2 * head)
        fold(pair[:, :head], pair[:, head:], kpos_ref[i])
        return carry

    lax.fori_loop(0, blocks // 2, step, 0)
    for h in range(heads):
        o_ref[:, h * head : (h + 1) * head] = (acc_ref[h] / l_ref[h]).astype(BF)


def attention(own, img, kv, kvi, index, qpos, qstart, kpos, ownpos, ipos, iown):
    rows = own.shape[0]
    head = kv.shape[2] // 2
    heads = (own.shape[1] - 2 * head) // head
    return pl.pallas_call(
        attention_kernel,
        out_shape=jax.ShapeDtypeStruct((rows, heads * head), BF),
        scratch_shapes=[
            pltpu.VMEM((heads, rows, 1), F32),
            pltpu.VMEM((heads, rows, 1), F32),
            pltpu.VMEM((heads, rows, head), F32),
        ],
        compiler_params=pltpu.CompilerParams(vmem_limit_bytes=MEM),
        name="attention",
    )(own, img, kv, kvi, index, qpos, qstart, kpos, ownpos, ipos, iown)


def output_kernel(core_ref, att_ref, tok_ref, img_ref, index_ref, own_ref, oth_ref, o_ref):
    step = pl.program_id(0)
    rows = tok_ref.shape[0]
    slots = img_ref.shape[0]
    tiles = own_ref.shape[1]
    lanes = own_ref.shape[3]
    index = index_ref[...]
    picker = (index == lax.broadcasted_iota(jnp.int32, (rows, slots), 1)).astype(F32).astype(BF)
    is_img = index < slots

    def body(w_ref):
        for t in range(0, tiles, 2):
            at = slice(t * lanes, (t + 2) * lanes)
            w = jnp.concatenate([w_ref[0, t], w_ref[0, t + 1]], axis=1)
            update = dot_f32(att_ref[...], w)
            base = jnp.where(is_img, dot_f32(picker, img_ref[:, at]), tok_ref[:, at].astype(F32))
            o_ref[:, at] = (base + update).astype(BF)

    @pl.when(step < 4)
    def _():
        body(own_ref)

    @pl.when(step >= 4)
    def _():
        body(oth_ref)


def output_layer(core, att, tokens, images, index, own, oth):
    rows, width = tokens.shape
    slots = images.shape[0]
    tiles, depth, lanes = own.shape[1:]
    half = tiles // 2
    cols = half * lanes

    def column(i, c):
        side = jnp.where(i < 4, c[0], 1 - c[0])
        return (0, ((i // 2) % 2) * 4 + side * 2 + i % 2)

    return pl.pallas_call(
        output_kernel,
        grid_spec=pltpu.PrefetchScalarGridSpec(
            num_scalar_prefetch=1,
            grid=(8,),
            in_specs=[
                pl.BlockSpec(att.shape, lambda i, c: (0, 0)),
                pl.BlockSpec((rows, cols), column),
                pl.BlockSpec((slots, cols), column),
                pl.BlockSpec((rows, 1), lambda i, c: (0, 0)),
                pl.BlockSpec(
                    (1, half, depth, lanes),
                    lambda i, c: (jnp.minimum(i, 3) // 2, jnp.minimum(i, 3) % 2, 0, 0),
                ),
                pl.BlockSpec(
                    (1, half, depth, lanes),
                    lambda i, c: (jnp.maximum(i - 4, 0) // 2, jnp.maximum(i - 4, 0) % 2, 0, 0),
                ),
            ],
            out_specs=pl.BlockSpec((rows, cols), column),
        ),
        out_shape=jax.ShapeDtypeStruct((rows, width), BF),
        compiler_params=pltpu.CompilerParams(vmem_limit_bytes=MEM),
        name="output_layer",
    )(core, att, tokens, images, index, own, oth)


def swap(x, axis):
    return lax.ppermute(x, axis, [(0, 1), (1, 0)])


def turns(x, axis):
    count = lax.axis_size(axis)
    me = lax.axis_index(axis)
    yield me, x
    for k in range(1, count):
        yield (me - k) % count, lax.ppermute(x, axis, [(i, (i + k) % count) for i in range(count)])


def gather_zy(x, first):
    nz, ny = (lax.axis_size(Z), lax.axis_size(Y))
    if first == Z:
        line = jnp.zeros((nz, 1) + x.shape, x.dtype)
        for at, part in turns(x, Z):
            line = lax.dynamic_update_slice_in_dim(line, part[None, None], at, 0)
        plane = jnp.zeros((nz, ny) + x.shape, x.dtype)
        for at, part in turns(line, Y):
            plane = lax.dynamic_update_slice_in_dim(plane, part, at, 1)
    else:
        line = jnp.zeros((1, ny) + x.shape, x.dtype)
        for at, part in turns(x, Y):
            line = lax.dynamic_update_slice_in_dim(line, part[None, None], at, 1)
        plane = jnp.zeros((nz, ny) + x.shape, x.dtype)
        for at, part in turns(line, Z):
            plane = lax.dynamic_update_slice_in_dim(plane, part, at, 0)
    return plane


def copies_to(x, axes):
    count = lax.axis_size(axes)
    return lax.all_to_all(jnp.broadcast_to(x[None], (count,) + x.shape), axes, 0, 0, tiled=True)


def partner_halves(x, axis, core):
    size = x.shape[axis] // 2
    mine = swap(lax.dynamic_slice_in_dim(x, core * size, size, axis), XHI)
    other = swap(mine, CORE)
    buffer = jnp.zeros_like(x)
    buffer = lax.dynamic_update_slice_in_dim(buffer, mine, core * size, axis)
    return lax.dynamic_update_slice_in_dim(buffer, other, (1 - core) * size, axis)


def keys_for_later(block, x_hi, zy):
    below = lax.ppermute(block, XHI, [(0, 1)])
    count = lax.axis_size(ZY)
    receiver = jnp.arange(count, dtype=jnp.int32)
    take_below = ((x_hi == 1) & (receiver <= zy)).reshape((count,) + (1,) * block.ndim)
    outgoing = jnp.where(take_below, below[None], block[None])
    return lax.all_to_all(outgoing, ZY, 0, 0, tiled=True)


def on_device(
    patches, piece_ids, vit_gain, vit_qkv, vit_out, merge_gain, merge_up, merge_down, dest,
    tokens, image_index, doc_lengths, attn_gain, attn_qkv, attn_out,
):
    core = lax.axis_index(CORE)
    x_hi = lax.axis_index(XHI)
    zy = lax.axis_index(ZY)
    y_odd = lax.axis_index(Y) % 2
    seq_count = lax.axis_size(SEQ)
    seq_index = lax.axis_index(SEQ)
    places = seq_count // 2
    tok_rows, width = tokens.shape
    core_arg = core.reshape(1).astype(jnp.int32)

    qkv_own = copies_to(attn_qkv, SAME_CORE)
    qkv_own = qkv_own.reshape(2, -1, attn_qkv.shape[1])
    qkv_oth = swap(qkv_own, CORE)

    depth, sliver = attn_out.shape
    upper, lower = (attn_out[: depth // 2], attn_out[depth // 2 :])
    give = jnp.where(y_odd == 1, upper, lower)
    keep = jnp.where(y_odd == 1, lower, upper)
    got = lax.ppermute(give, Y, [(0, 1), (1, 0), (2, 3), (3, 2)])
    tile = jnp.where(
        y_odd == 1, jnp.concatenate([got, keep], axis=1), jnp.concatenate([keep, got], axis=1)
    )
    out_own = lax.all_gather(tile, SAME_CORE, axis=0, tiled=False)
    out_own = out_own.reshape(2, -1, depth, 2 * sliver)
    out_oth = swap(out_own, CORE)

    up_own = merge_up.T
    up_oth = partner_halves(up_own, 1, core)
    down_oth = partner_halves(merge_down, 0, core)

    merge_in = window_layer(patches, piece_ids, vit_gain, vit_qkv, vit_out, merge_gain)
    own_rows = merge_in.shape[0]
    half = merge_in.shape[1] // 2
    note = jnp.broadcast_to(dest.astype(BF)[:, None], (own_rows, 128))
    part_a = gather_zy(jnp.concatenate([merge_in[:, :half], note], axis=1), Z)
    part_b = gather_zy(merge_in[:, half:], Y)
    part_a = part_a.reshape(places * own_rows, half + 128)
    part_b = part_b.reshape(places * own_rows, half)
    targets = part_a[:, half].astype(jnp.int32)

    def hidden(weights):
        total = dot_f32(weights[:, :half], part_a[:, :half], 1, 1) + dot_f32(weights[:, half:], part_b, 1, 1)
        return jax.nn.gelu(total, approximate=False).astype(BF)

    mine, theirs = (hidden(up_own), hidden(up_oth))
    hidden_0 = gather_zy(jnp.where(x_hi == 0, mine, theirs), Z).reshape(-1, places * own_rows)
    hidden_1 = gather_zy(jnp.where(x_hi == 0, theirs, mine), Y).reshape(-1, places * own_rows)
    middle = hidden_0.shape[0]

    def columns(weights):
        return (
            dot_f32(hidden_0, weights[:middle], 0, 0) + dot_f32(hidden_1, weights[middle:], 0, 0)
        ).astype(BF)

    mine, theirs = (columns(merge_down), columns(down_oth))
    merged = jnp.concatenate(
        [jnp.where(x_hi == 0, mine, theirs), jnp.where(x_hi == 0, theirs, mine)], axis=1
    )

    receivers = jnp.arange(seq_count, dtype=jnp.int32)
    row_home = jnp.arange(places * own_rows, dtype=jnp.int32) // own_rows
    homes = jnp.arange(places, dtype=jnp.int32)
    select = (targets[None, None, :] == receivers[:, None, None]) & (
        row_home[None, None, :] == homes[None, :, None]
    )
    outgoing = dot_f32(select.astype(BF).reshape(seq_count * places, -1), merged).astype(BF)
    arrived = lax.all_to_all(
        outgoing.reshape(seq_count, places, -1), SEQ, split_axis=0, concat_axis=0, tiled=True
    )
    arrived = arrived.reshape(2, places, places, 2, -1)
    images = arrived.transpose(0, 2, 3, 1, 4).reshape(seq_count, width)

    proj_text = project(core_arg, tokens, attn_gain, qkv_own, qkv_oth)
    query_width = depth
    index_row = jnp.broadcast_to(image_index.astype(BF)[None, :], (16, tok_rows))
    block = jnp.concatenate([proj_text[:, query_width:], index_row], axis=0)
    kv_text = keys_for_later(block, x_hi, zy)

    proj_img = project(core_arg, images, attn_gain, qkv_own, qkv_oth)
    kv_img = keys_for_later(proj_img[:, query_width:], x_hi, zy)

    positions = seq_index * tok_rows + jnp.arange(tok_rows, dtype=jnp.int32)
    lengths = doc_lengths[0]
    order_of = jnp.arange(lengths.shape[0], dtype=jnp.int32)
    starts = jnp.sum(jnp.where(order_of[None, :] < order_of[:, None], lengths[None, :], 0), axis=1)
    doc_start = jnp.max(jnp.where(starts[None, :] <= positions[:, None], starts[None, :], 0), axis=1)
    slot_ids = jnp.arange(seq_count, dtype=jnp.int32)
    within = jnp.arange(tok_rows, dtype=jnp.int32)
    home = jnp.where(x_hi == 0, homes, jnp.where(homes >= zy, homes, homes + places))
    useful = (x_hi == 1) | (homes < zy)
    indexes = kv_text[:, tok_rows, :].astype(jnp.int32)
    kpos = jnp.where(
        (indexes == seq_count) & useful[:, None], home[:, None] * tok_rows + within[None, :], FAR
    )
    ownpos = jnp.where(image_index == seq_count, positions, FAR)
    hits = indexes[:, None, :] == slot_ids[None, :, None]
    ipos = jnp.min(
        jnp.where(hits & useful[:, None, None], (home[:, None] * tok_rows + within[None, :])[:, None, :], FAR),
        axis=-1,
    )
    iown = jnp.min(
        jnp.where(image_index[None, :] == slot_ids[:, None], positions[None, :], FAR), axis=-1
    )

    index_col = image_index.reshape(tok_rows, 1)
    attended = attention(
        proj_text,
        proj_img,
        kv_text,
        kv_img.reshape(-1, kv_img.shape[2]),
        index_col,
        positions.reshape(tok_rows, 1),
        doc_start.reshape(tok_rows, 1),
        kpos.reshape(places // 2, 1, 2 * tok_rows),
        ownpos.reshape(1, tok_rows),
        ipos.reshape(1, -1),
        iown.reshape(1, -1),
    )
    return output_layer(core_arg, attended, tokens, images, index_col, out_own, out_oth)


def solution(mesh):
    torus = Mesh(mesh.devices.reshape(2, 2, 2, 4, 4), GRP_SEQ)
    return jax.shard_map(
        on_device,
        mesh=torus,
        in_specs=(
            P(GRP_SEQ, None),
            P(GRP_SEQ, None),
            P(),
            P(),
            P(),
            P(),
            P(None, SEQ),
            P(None, SEQ),
            P(GRP_SEQ),
            P(GRP_SEQ, None),
            P(GRP_SEQ),
            P(GRP, None),
            P(),
            P(GRP_SEQ, None),
            P(None, GRP_SEQ),
        ),
        out_specs=P(GRP_SEQ, None),
        check_vma=False,
    )
```

```python
import jax
import jax.numpy as jnp
from jax import lax
from jax.experimental import pallas as pl
from jax.experimental.pallas import tpu as pltpu
from jax.sharding import Mesh
from jax.sharding import PartitionSpec as P

VHEADS = 16
XLO, CORE, XHI, Z, Y = ("grp_0", "grp_1", "seq_0", "seq_1", "seq_2")
SEQ = (XHI, Z, Y)
ZY = (Z, Y)
GRP_SEQ = (XLO, CORE, XHI, Z, Y)
GRP = (XLO, CORE)
EPSILON = 1e-06
NEG = -1e30
FAR = 1 << 30
BF = jnp.bfloat16
F32 = jnp.float32
MEM = 56 * 1024 * 1024


def dot_f32(a, b, ca=1, cb=0):
    return lax.dot_general(a, b, (((ca,), (cb,)), ((), ())), preferred_element_type=F32)


def window_kernel(x_ref, prow_ref, pcol_ref, gain_ref, w_ref, wo_ref, mgain_ref, o_ref, n_ref, p_ref):
    step = pl.program_id(0)
    rows, feats = x_ref.shape
    head = feats // VHEADS

    @pl.when(step == 0)
    def _():
        x = x_ref[...].astype(F32)
        mean = jnp.mean(x * x, axis=-1, keepdims=True)
        n_ref[...] = (x * lax.rsqrt(mean + EPSILON) * gain_ref[...]).astype(BF)

    for part in range(3):

        @pl.when(step == part)
        def _(part=part):
            p_ref[part] = dot_f32(n_ref[...], w_ref[...]).astype(BF)

    @pl.when(step == 2)
    def _():
        q, k, v = (p_ref[0], p_ref[1], p_ref[2])
        lane = lax.broadcasted_iota(jnp.int32, (rows, feats), 1)
        same = pcol_ref[...] == prow_ref[...]
        mixed = jnp.zeros((rows, feats), F32)
        for h in range(VHEADS):
            mine = (lane >= h * head) & (lane < (h + 1) * head)
            s = dot_f32(jnp.where(mine, q, jnp.zeros_like(q)), k, 1, 1) * head ** (-0.5)
            s = jnp.where(same, s, NEG)
            w = jnp.exp(s - jnp.max(s, axis=-1, keepdims=True))
            total = jnp.sum(w, axis=-1, keepdims=True)
            mixed = jnp.where(mine, dot_f32(w.astype(BF), v) / total, mixed)
        resid = x_ref[...].astype(F32) + dot_f32(mixed.astype(BF), wo_ref[...])
        mean = jnp.mean(resid * resid, axis=-1, keepdims=True)
        merged = (resid * lax.rsqrt(mean + EPSILON) * mgain_ref[...]).astype(BF)
        r_out = lax.broadcasted_iota(jnp.int32, (rows // 4, rows), 0)
        r_in = lax.broadcasted_iota(jnp.int32, (rows // 4, rows), 1)
        for j in range(4):
            pick = jnp.where(r_in == 4 * r_out + j, 1.0, 0.0).astype(BF)
            o_ref[:, j * feats : (j + 1) * feats] = dot_f32(pick, merged).astype(BF)


def window_layer(patches, piece_ids, vit_gain, vit_qkv, vit_out, merge_gain):
    rows, feats = patches.shape
    whole = lambda *shape: pl.BlockSpec(shape, lambda i: (0,) * len(shape))
    return pl.pallas_call(
        window_kernel,
        grid=(3,),
        in_specs=[
            whole(rows, feats),
            whole(1, rows),
            whole(rows, 1),
            whole(1, feats),
            pl.BlockSpec((feats, feats), lambda i: (0, i)),
            whole(feats, feats),
            whole(1, feats),
        ],
        out_specs=whole(rows // 4, 4 * feats),
        out_shape=jax.ShapeDtypeStruct((rows // 4, 4 * feats), BF),
        scratch_shapes=[pltpu.VMEM((rows, feats), BF), pltpu.VMEM((3, rows, feats), BF)],
        compiler_params=pltpu.CompilerParams(vmem_limit_bytes=MEM),
        name="window_layer",
    )(
        patches,
        piece_ids.reshape(1, rows),
        piece_ids.reshape(rows, 1),
        vit_gain.reshape(1, feats),
        vit_qkv,
        vit_out,
        merge_gain.reshape(1, feats),
    )


def project_kernel(place_ref, x_ref, gain_ref, *refs):
    w_refs, (o_ref, buf_ref, sem_ref) = (refs[:-3], refs[-3:])
    rows, width = x_ref.shape
    depth = buf_ref.shape[1]
    loads = [pltpu.make_async_copy(w, buf_ref.at[i], sem_ref.at[i]) for i, w in enumerate(w_refs)]
    for load in loads:
        load.start()
    total = jnp.zeros((rows, 1), F32)
    for c in range(0, width, depth):
        x = x_ref[:, c : c + depth].astype(F32)
        total = total + jnp.sum(x * x, axis=-1, keepdims=True)
    scale = lax.rsqrt(total / width + EPSILON)
    acc = jnp.zeros(o_ref.shape, F32)
    for i, load in enumerate(loads):
        start = pl.multiple_of(place_ref[i] * depth, depth)
        x = x_ref[:, pl.ds(start, depth)].astype(F32)
        n = (x * scale * gain_ref[:, pl.ds(start, depth)]).astype(BF)
        load.wait()
        acc = acc + dot_f32(n, buf_ref[i])
    o_ref[...] = acc.astype(BF)


def project(place, x, gain, parts):
    rows, width = x.shape
    depth, cols = parts[0].shape
    return pl.pallas_call(
        project_kernel,
        grid_spec=pltpu.PrefetchScalarGridSpec(
            num_scalar_prefetch=1,
            grid=(1,),
            in_specs=[
                pl.BlockSpec((rows, width), lambda i, c: (0, 0)),
                pl.BlockSpec((1, width), lambda i, c: (0, 0)),
            ]
            + [pl.BlockSpec(memory_space=pl.ANY)] * len(parts),
            out_specs=pl.BlockSpec((rows, cols), lambda i, c: (0, 0)),
            scratch_shapes=[
                pltpu.VMEM((len(parts), depth, cols), BF),
                pltpu.SemaphoreType.DMA((len(parts),)),
            ],
        ),
        out_shape=jax.ShapeDtypeStruct((rows, cols), BF),
        compiler_params=pltpu.CompilerParams(vmem_limit_bytes=MEM),
        name="project",
    )(place, x, gain.reshape(1, width), *parts)


def attention_kernel(
    own_ref, img_ref, kv_ref, kvi_ref, index_ref, qpos_ref, qstart_ref, kpos_ref, ownpos_ref, ipos_ref, iown_ref,
    o_ref, m_ref, l_ref, acc_ref,
):
    rows = own_ref.shape[0]
    slots = img_ref.shape[0]
    head = kv_ref.shape[2] // 2
    heads = o_ref.shape[1] // head
    width = heads * head
    blocks = kv_ref.shape[0]
    m_ref[...] = jnp.full_like(m_ref, NEG)
    l_ref[...] = jnp.zeros_like(l_ref)
    acc_ref[...] = jnp.zeros_like(acc_ref)
    index = index_ref[...]
    picker = (index == lax.broadcasted_iota(jnp.int32, (rows, slots), 1)).astype(F32).astype(BF)
    is_img = index < slots
    queries = [
        jnp.where(
            is_img,
            dot_f32(picker, img_ref[:, h * head : (h + 1) * head]),
            own_ref[:, h * head : (h + 1) * head].astype(F32),
        ).astype(BF)
        for h in range(heads)
    ]
    qpos, qstart = (qpos_ref[...], qstart_ref[...])
    scale = head ** (-0.5)

    def fold(keys, values, kpos):
        allowed = (kpos >= qstart) & (kpos <= qpos)
        for h in range(heads):
            s = jnp.where(allowed, dot_f32(queries[h], keys, 1, 1) * scale, NEG)
            old = m_ref[h]
            new = jnp.maximum(old, jnp.max(s, axis=-1, keepdims=True))
            shrink = jnp.exp(old - new)
            w = jnp.exp(s - new)
            l_ref[h] = l_ref[h] * shrink + jnp.sum(w, axis=-1, keepdims=True)
            acc_ref[h] = acc_ref[h] * shrink + dot_f32(w.astype(BF), values)
            m_ref[h] = new

    fold(own_ref[:, width : width + head], own_ref[:, width + head :], ownpos_ref[...])
    fold(img_ref[:, width : width + head], img_ref[:, width + head :], iown_ref[...])
    fold(kvi_ref[:, :head], kvi_ref[:, head:], ipos_ref[...])

    def step(i, carry):
        pair = kv_ref[pl.ds(2 * i, 2), :rows, :].reshape(2 * rows, 2 * head)
        fold(pair[:, :head], pair[:, head:], kpos_ref[i])
        return carry

    lax.fori_loop(0, blocks // 2, step, 0)
    for h in range(heads):
        o_ref[:, h * head : (h + 1) * head] = (acc_ref[h] / l_ref[h]).astype(BF)


def attention(own, img, kv, kvi, index, qpos, qstart, kpos, ownpos, ipos, iown):
    rows = own.shape[0]
    head = kv.shape[2] // 2
    heads = (own.shape[1] - 2 * head) // head
    return pl.pallas_call(
        attention_kernel,
        out_shape=jax.ShapeDtypeStruct((rows, heads * head), BF),
        scratch_shapes=[
            pltpu.VMEM((heads, rows, 1), F32),
            pltpu.VMEM((heads, rows, 1), F32),
            pltpu.VMEM((heads, rows, head), F32),
        ],
        compiler_params=pltpu.CompilerParams(vmem_limit_bytes=MEM),
        name="attention",
    )(own, img, kv, kvi, index, qpos, qstart, kpos, ownpos, ipos, iown)


def output_kernel(place_ref, att_ref, tok_ref, img_ref, index_ref, *refs):
    w_refs, (o_ref, buf_ref, sem_ref) = (refs[:-3], refs[-3:])
    step = pl.program_id(0)
    rows = tok_ref.shape[0]
    slots = img_ref.shape[0]
    tiles, _, lanes = buf_ref.shape[1:]
    index = index_ref[...]
    picker = (index == lax.broadcasted_iota(jnp.int32, (rows, slots), 1)).astype(F32).astype(BF)
    is_img = index < slots
    loads = [pltpu.make_async_copy(w, buf_ref.at[i], sem_ref.at[i]) for i, w in enumerate(w_refs)]

    @pl.when(step == 0)
    def _():
        for load in loads:
            load.start()

    for i, load in enumerate(loads):

        @pl.when(step == i)
        def _(load=load):
            load.wait()

    for t in range(0, tiles, 2):
        at = slice(t * lanes, (t + 2) * lanes)
        w = jnp.concatenate([buf_ref[step, t], buf_ref[step, t + 1]], axis=1)
        update = dot_f32(att_ref[...], w)
        base = jnp.where(is_img, dot_f32(picker, img_ref[:, at]), tok_ref[:, at].astype(F32))
        o_ref[:, at] = (base + update).astype(BF)


def output_layer(place, att, tokens, images, index, parts):
    rows, width = tokens.shape
    slots = images.shape[0]
    tiles, depth, lanes = parts[0].shape
    cols = tiles * lanes
    column = lambda i, c: (0, c[i])
    return pl.pallas_call(
        output_kernel,
        grid_spec=pltpu.PrefetchScalarGridSpec(
            num_scalar_prefetch=1,
            grid=(len(parts),),
            in_specs=[
                pl.BlockSpec(att.shape, lambda i, c: (0, 0)),
                pl.BlockSpec((rows, cols), column),
                pl.BlockSpec((slots, cols), column),
                pl.BlockSpec((rows, 1), lambda i, c: (0, 0)),
            ]
            + [pl.BlockSpec(memory_space=pl.ANY)] * len(parts),
            out_specs=pl.BlockSpec((rows, cols), column),
            scratch_shapes=[
                pltpu.VMEM((len(parts), tiles, depth, lanes), BF),
                pltpu.SemaphoreType.DMA((len(parts),)),
            ],
        ),
        out_shape=jax.ShapeDtypeStruct((rows, width), BF),
        compiler_params=pltpu.CompilerParams(vmem_limit_bytes=MEM),
        name="output_layer",
    )(place, att, tokens, images, index, *parts)


def swap(x, axis):
    return lax.ppermute(x, axis, [(0, 1), (1, 0)])


def turns(x, axis):
    count = lax.axis_size(axis)
    me = lax.axis_index(axis)
    yield me, x
    for k in range(1, count):
        yield (me - k) % count, lax.ppermute(x, axis, [(i, (i + k) % count) for i in range(count)])


def gather_zy(x, first):
    nz, ny = (lax.axis_size(Z), lax.axis_size(Y))
    if first == Z:
        line = jnp.zeros((nz, 1) + x.shape, x.dtype)
        for at, part in turns(x, Z):
            line = lax.dynamic_update_slice_in_dim(line, part[None, None], at, 0)
        plane = jnp.zeros((nz, ny) + x.shape, x.dtype)
        for at, part in turns(line, Y):
            plane = lax.dynamic_update_slice_in_dim(plane, part, at, 1)
    else:
        line = jnp.zeros((1, ny) + x.shape, x.dtype)
        for at, part in turns(x, Y):
            line = lax.dynamic_update_slice_in_dim(line, part[None, None], at, 1)
        plane = jnp.zeros((nz, ny) + x.shape, x.dtype)
        for at, part in turns(line, Z):
            plane = lax.dynamic_update_slice_in_dim(plane, part, at, 0)
    return plane


def after(x, *others):
    return lax.optimization_barrier((x, *others))[0]


def along_x(x, steps):
    place = lambda at: (at % 2) * 2 + at // 2
    return lax.ppermute(x, (XLO, XHI), [(place(at), place((at + steps) % 4)) for at in range(4)])


def around_x(x):
    parts = [x] + [along_x(x, steps) for steps in (1, 3, 2)]
    return parts + [swap(part, CORE) for part in parts]


def copies_to(x, axes):
    count = lax.axis_size(axes)
    return lax.all_to_all(jnp.broadcast_to(x[None], (count,) + x.shape), axes, 0, 0, tiled=True)


def partner_halves(x, axis, core):
    size = x.shape[axis] // 2
    mine = swap(lax.dynamic_slice_in_dim(x, core * size, size, axis), XHI)
    other = swap(mine, CORE)
    buffer = jnp.zeros_like(x)
    buffer = lax.dynamic_update_slice_in_dim(buffer, mine, core * size, axis)
    return lax.dynamic_update_slice_in_dim(buffer, other, (1 - core) * size, axis)


def keys_for_later(block, x_hi, zy):
    below = lax.ppermute(block, XHI, [(0, 1)])
    count = lax.axis_size(ZY)
    receiver = jnp.arange(count, dtype=jnp.int32)
    take_below = ((x_hi == 1) & (receiver <= zy)).reshape((count,) + (1,) * block.ndim)
    outgoing = jnp.where(take_below, below[None], block[None])
    return lax.all_to_all(outgoing, ZY, 0, 0, tiled=True)


def on_device(
    patches, piece_ids, vit_gain, vit_qkv, vit_out, merge_gain, merge_up, merge_down, dest,
    tokens, image_index, doc_lengths, attn_gain, attn_qkv, attn_out,
):
    core = lax.axis_index(CORE)
    x_hi = lax.axis_index(XHI)
    zy = lax.axis_index(ZY)
    y_odd = lax.axis_index(Y) % 2
    seq_count = lax.axis_size(SEQ)
    seq_index = lax.axis_index(SEQ)
    places = seq_count // 2
    tok_rows, width = tokens.shape

    depth, sliver = attn_out.shape
    upper, lower = (attn_out[: depth // 2], attn_out[depth // 2 :])
    give = jnp.where(y_odd == 1, upper, lower)
    keep = jnp.where(y_odd == 1, lower, upper)
    got = lax.ppermute(give, Y, [(0, 1), (1, 0), (2, 3), (3, 2)])
    tile = jnp.where(
        y_odd == 1, jnp.concatenate([got, keep], axis=1), jnp.concatenate([keep, got], axis=1)
    )
    spread = copies_to(attn_qkv, ZY)
    qkv_parts = around_x(spread.reshape(-1, attn_qkv.shape[1]))
    spread = copies_to(after(tile, spread), ZY)
    out_parts = around_x(after(spread.reshape(-1, depth, 2 * sliver), qkv_parts[3]))
    chip_x = x_hi * 2 + lax.axis_index(XLO)
    place = [
        (source % 2) * 4 + side * 2 + source // 2
        for side in (core, 1 - core)
        for source in [(chip_x - steps) % 4 for steps in (0, 1, 3, 2)]
    ]
    place = jnp.stack(place).astype(jnp.int32)

    up_own = merge_up.T
    up_oth = partner_halves(up_own, 1, core)
    down_oth = partner_halves(merge_down, 0, core)

    merge_in = window_layer(patches, piece_ids, vit_gain, vit_qkv, vit_out, merge_gain)
    own_rows = merge_in.shape[0]
    half = merge_in.shape[1] // 2
    note = jnp.broadcast_to(dest.astype(BF)[:, None], (own_rows, 128))
    part_a = gather_zy(jnp.concatenate([merge_in[:, :half], note], axis=1), Z)
    part_b = gather_zy(merge_in[:, half:], Y)
    part_a = part_a.reshape(places * own_rows, half + 128)
    part_b = part_b.reshape(places * own_rows, half)
    targets = part_a[:, half].astype(jnp.int32)

    def hidden(weights):
        total = dot_f32(weights[:, :half], part_a[:, :half], 1, 1) + dot_f32(weights[:, half:], part_b, 1, 1)
        return jax.nn.gelu(total, approximate=False).astype(BF)

    mine, theirs = (hidden(up_own), hidden(up_oth))
    hidden_0 = gather_zy(jnp.where(x_hi == 0, mine, theirs), Z).reshape(-1, places * own_rows)
    hidden_1 = gather_zy(jnp.where(x_hi == 0, theirs, mine), Y).reshape(-1, places * own_rows)
    middle = hidden_0.shape[0]
    hidden_1 = after(hidden_1, out_parts[1])

    proj_text = project(place, tokens, attn_gain, qkv_parts)
    query_width = depth
    index_row = jnp.broadcast_to(image_index.astype(BF)[None, :], (16, tok_rows))
    block = jnp.concatenate([proj_text[:, query_width:], index_row], axis=0)
    block = after(block, *out_parts[2:4])
    kv_text = keys_for_later(block, x_hi, zy)

    def columns(weights):
        return (
            dot_f32(hidden_0, weights[:middle], 0, 0) + dot_f32(hidden_1, weights[middle:], 0, 0)
        ).astype(BF)

    mine, theirs = (columns(merge_down), columns(down_oth))
    merged = jnp.concatenate(
        [jnp.where(x_hi == 0, mine, theirs), jnp.where(x_hi == 0, theirs, mine)], axis=1
    )

    receivers = jnp.arange(seq_count, dtype=jnp.int32)
    row_home = jnp.arange(places * own_rows, dtype=jnp.int32) // own_rows
    homes = jnp.arange(places, dtype=jnp.int32)
    select = (targets[None, None, :] == receivers[:, None, None]) & (
        row_home[None, None, :] == homes[None, :, None]
    )
    outgoing = dot_f32(select.astype(BF).reshape(seq_count * places, -1), merged).astype(BF)
    arrived = lax.all_to_all(
        outgoing.reshape(seq_count, places, -1), SEQ, split_axis=0, concat_axis=0, tiled=True
    )
    arrived = arrived.reshape(2, places, places, 2, -1)
    images = arrived.transpose(0, 2, 3, 1, 4).reshape(seq_count, width)

    proj_img = project(place, images, attn_gain, qkv_parts)
    kv_img = keys_for_later(proj_img[:, query_width:], x_hi, zy)

    positions = seq_index * tok_rows + jnp.arange(tok_rows, dtype=jnp.int32)
    lengths = doc_lengths[0]
    order_of = jnp.arange(lengths.shape[0], dtype=jnp.int32)
    starts = jnp.sum(jnp.where(order_of[None, :] < order_of[:, None], lengths[None, :], 0), axis=1)
    doc_start = jnp.max(jnp.where(starts[None, :] <= positions[:, None], starts[None, :], 0), axis=1)
    slot_ids = jnp.arange(seq_count, dtype=jnp.int32)
    within = jnp.arange(tok_rows, dtype=jnp.int32)
    home = jnp.where(x_hi == 0, homes, jnp.where(homes >= zy, homes, homes + places))
    useful = (x_hi == 1) | (homes < zy)
    indexes = kv_text[:, tok_rows, :].astype(jnp.int32)
    kpos = jnp.where(
        (indexes == seq_count) & useful[:, None], home[:, None] * tok_rows + within[None, :], FAR
    )
    ownpos = jnp.where(image_index == seq_count, positions, FAR)
    hits = indexes[:, None, :] == slot_ids[None, :, None]
    ipos = jnp.min(
        jnp.where(hits & useful[:, None, None], (home[:, None] * tok_rows + within[None, :])[:, None, :], FAR),
        axis=-1,
    )
    iown = jnp.min(
        jnp.where(image_index[None, :] == slot_ids[:, None], positions[None, :], FAR), axis=-1
    )

    index_col = image_index.reshape(tok_rows, 1)
    attended = attention(
        proj_text,
        proj_img,
        kv_text,
        kv_img.reshape(-1, kv_img.shape[2]),
        index_col,
        positions.reshape(tok_rows, 1),
        doc_start.reshape(tok_rows, 1),
        kpos.reshape(places // 2, 1, 2 * tok_rows),
        ownpos.reshape(1, tok_rows),
        ipos.reshape(1, -1),
        iown.reshape(1, -1),
    )
    return output_layer(place, attended, tokens, images, index_col, out_parts)


def solution(mesh):
    torus = Mesh(mesh.devices.reshape(2, 2, 2, 4, 4), GRP_SEQ)
    return jax.shard_map(
        on_device,
        mesh=torus,
        in_specs=(
            P(GRP_SEQ, None),
            P(GRP_SEQ, None),
            P(),
            P(),
            P(),
            P(),
            P(None, SEQ),
            P(None, SEQ),
            P(GRP_SEQ),
            P(GRP_SEQ, None),
            P(GRP_SEQ),
            P(GRP, None),
            P(),
            P(GRP_SEQ, None),
            P(None, GRP_SEQ),
        ),
        out_specs=P(GRP_SEQ, None),
        check_vma=False,
    )
```

```python
import jax
import jax.numpy as jnp
from jax import lax
from jax.experimental import pallas as pl
from jax.experimental.pallas import tpu as pltpu
from jax.sharding import Mesh
from jax.sharding import PartitionSpec as P

VHEADS = 16
XLO, CORE, XHI, Z, Y = ("grp_0", "grp_1", "seq_0", "seq_1", "seq_2")
SEQ = (XHI, Z, Y)
ZY = (Z, Y)
GRP_SEQ = (XLO, CORE, XHI, Z, Y)
GRP = (XLO, CORE)
EPSILON = 1e-06
NEG = -1e30
FAR = 1 << 30
BF = jnp.bfloat16
F32 = jnp.float32
MEM = 56 * 1024 * 1024


def dot_f32(a, b, ca=1, cb=0):
    return lax.dot_general(a, b, (((ca,), (cb,)), ((), ())), preferred_element_type=F32)


def window_kernel(x_ref, prow_ref, pcol_ref, gain_ref, w_ref, wo_ref, mgain_ref, o_ref, n_ref, p_ref):
    step = pl.program_id(0)
    rows, feats = x_ref.shape
    head = feats // VHEADS

    @pl.when(step == 0)
    def _():
        x = x_ref[...].astype(F32)
        mean = jnp.mean(x * x, axis=-1, keepdims=True)
        n_ref[...] = (x * lax.rsqrt(mean + EPSILON) * gain_ref[...]).astype(BF)

    for part in range(3):

        @pl.when(step == part)
        def _(part=part):
            p_ref[part] = dot_f32(n_ref[...], w_ref[...]).astype(BF)

    @pl.when(step == 2)
    def _():
        q, k, v = (p_ref[0], p_ref[1], p_ref[2])
        lane = lax.broadcasted_iota(jnp.int32, (rows, feats), 1)
        same = pcol_ref[...] == prow_ref[...]
        mixed = jnp.zeros((rows, feats), F32)
        for h in range(VHEADS):
            mine = (lane >= h * head) & (lane < (h + 1) * head)
            s = dot_f32(jnp.where(mine, q, jnp.zeros_like(q)), k, 1, 1) * head ** (-0.5)
            s = jnp.where(same, s, NEG)
            w = jnp.exp(s - jnp.max(s, axis=-1, keepdims=True))
            total = jnp.sum(w, axis=-1, keepdims=True)
            mixed = jnp.where(mine, dot_f32(w.astype(BF), v) / total, mixed)
        resid = x_ref[...].astype(F32) + dot_f32(mixed.astype(BF), wo_ref[...])
        mean = jnp.mean(resid * resid, axis=-1, keepdims=True)
        merged = (resid * lax.rsqrt(mean + EPSILON) * mgain_ref[...]).astype(BF)
        r_out = lax.broadcasted_iota(jnp.int32, (rows // 4, rows), 0)
        r_in = lax.broadcasted_iota(jnp.int32, (rows // 4, rows), 1)
        for j in range(4):
            pick = jnp.where(r_in == 4 * r_out + j, 1.0, 0.0).astype(BF)
            o_ref[:, j * feats : (j + 1) * feats] = dot_f32(pick, merged).astype(BF)


def window_layer(patches, piece_ids, vit_gain, vit_qkv, vit_out, merge_gain):
    rows, feats = patches.shape
    whole = lambda *shape: pl.BlockSpec(shape, lambda i: (0,) * len(shape))
    return pl.pallas_call(
        window_kernel,
        grid=(3,),
        in_specs=[
            whole(rows, feats),
            whole(1, rows),
            whole(rows, 1),
            whole(1, feats),
            pl.BlockSpec((feats, feats), lambda i: (0, i)),
            whole(feats, feats),
            whole(1, feats),
        ],
        out_specs=whole(rows // 4, 4 * feats),
        out_shape=jax.ShapeDtypeStruct((rows // 4, 4 * feats), BF),
        scratch_shapes=[pltpu.VMEM((rows, feats), BF), pltpu.VMEM((3, rows, feats), BF)],
        compiler_params=pltpu.CompilerParams(vmem_limit_bytes=MEM),
        name="window_layer",
    )(
        patches,
        piece_ids.reshape(1, rows),
        piece_ids.reshape(rows, 1),
        vit_gain.reshape(1, feats),
        vit_qkv,
        vit_out,
        merge_gain.reshape(1, feats),
    )


def piece_loads(refs, buf_ref, sem_ref):
    half = buf_ref.shape[1] // 2
    loads = []
    for side in range(2):
        own = refs[side * 5 : side * 5 + 5]
        for k in range(4):
            slot = side * 4 + k
            if k < 3:
                spots = [(own[k], buf_ref.at[slot])]
            else:
                spots = [(own[3 + i], buf_ref.at[slot, pl.ds(i * half, half)]) for i in range(2)]
            loads.append(
                [pltpu.make_async_copy(w, spot, sem_ref.at[side * 5 + k + i]) for i, (w, spot) in enumerate(spots)]
            )
    return loads


def project_kernel(place_ref, x_ref, gain_ref, *refs):
    w_refs, (o_ref, buf_ref, sem_ref) = (refs[:-3], refs[-3:])
    rows, width = x_ref.shape
    depth = buf_ref.shape[1]
    loads = piece_loads(w_refs, buf_ref, sem_ref)
    for load in loads:
        for copy in load:
            copy.start()
    total = jnp.zeros((rows, 1), F32)
    for c in range(0, width, depth):
        x = x_ref[:, c : c + depth].astype(F32)
        total = total + jnp.sum(x * x, axis=-1, keepdims=True)
    scale = lax.rsqrt(total / width + EPSILON)
    acc = jnp.zeros(o_ref.shape, F32)
    for i, load in enumerate(loads):
        start = pl.multiple_of(place_ref[i] * depth, depth)
        x = x_ref[:, pl.ds(start, depth)].astype(F32)
        n = (x * scale * gain_ref[:, pl.ds(start, depth)]).astype(BF)
        for copy in load:
            copy.wait()
        acc = acc + dot_f32(n, buf_ref[i])
    o_ref[...] = acc.astype(BF)


def project(place, x, gain, parts):
    rows, width = x.shape
    depth, cols = parts[0].shape
    return pl.pallas_call(
        project_kernel,
        grid_spec=pltpu.PrefetchScalarGridSpec(
            num_scalar_prefetch=1,
            grid=(1,),
            in_specs=[
                pl.BlockSpec((rows, width), lambda i, c: (0, 0)),
                pl.BlockSpec((1, width), lambda i, c: (0, 0)),
            ]
            + [pl.BlockSpec(memory_space=pl.ANY)] * len(parts),
            out_specs=pl.BlockSpec((rows, cols), lambda i, c: (0, 0)),
            scratch_shapes=[
                pltpu.VMEM((8, depth, cols), BF),
                pltpu.SemaphoreType.DMA((len(parts),)),
            ],
        ),
        out_shape=jax.ShapeDtypeStruct((rows, cols), BF),
        compiler_params=pltpu.CompilerParams(vmem_limit_bytes=MEM),
        name="project",
    )(place, x, gain.reshape(1, width), *parts)


def attention_kernel(
    own_ref, img_ref, kv_ref, kvi_ref, index_ref, qpos_ref, qstart_ref, kpos_ref, ownpos_ref, ipos_ref, iown_ref,
    o_ref, m_ref, l_ref, acc_ref,
):
    rows = own_ref.shape[0]
    slots = img_ref.shape[0]
    head = kv_ref.shape[2] // 2
    heads = o_ref.shape[1] // head
    width = heads * head
    blocks = kv_ref.shape[0]
    m_ref[...] = jnp.full_like(m_ref, NEG)
    l_ref[...] = jnp.zeros_like(l_ref)
    acc_ref[...] = jnp.zeros_like(acc_ref)
    index = index_ref[...]
    picker = (index == lax.broadcasted_iota(jnp.int32, (rows, slots), 1)).astype(F32).astype(BF)
    is_img = index < slots
    queries = [
        jnp.where(
            is_img,
            dot_f32(picker, img_ref[:, h * head : (h + 1) * head]),
            own_ref[:, h * head : (h + 1) * head].astype(F32),
        ).astype(BF)
        for h in range(heads)
    ]
    qpos, qstart = (qpos_ref[...], qstart_ref[...])
    scale = head ** (-0.5)

    def fold(keys, values, kpos):
        allowed = (kpos >= qstart) & (kpos <= qpos)
        for h in range(heads):
            s = jnp.where(allowed, dot_f32(queries[h], keys, 1, 1) * scale, NEG)
            old = m_ref[h]
            new = jnp.maximum(old, jnp.max(s, axis=-1, keepdims=True))
            shrink = jnp.exp(old - new)
            w = jnp.exp(s - new)
            l_ref[h] = l_ref[h] * shrink + jnp.sum(w, axis=-1, keepdims=True)
            acc_ref[h] = acc_ref[h] * shrink + dot_f32(w.astype(BF), values)
            m_ref[h] = new

    fold(own_ref[:, width : width + head], own_ref[:, width + head :], ownpos_ref[...])
    fold(img_ref[:, width : width + head], img_ref[:, width + head :], iown_ref[...])
    fold(kvi_ref[:, :head], kvi_ref[:, head:], ipos_ref[...])

    def step(i, carry):
        pair = kv_ref[pl.ds(2 * i, 2), :rows, :].reshape(2 * rows, 2 * head)
        fold(pair[:, :head], pair[:, head:], kpos_ref[i])
        return carry

    lax.fori_loop(0, blocks // 2, step, 0)
    for h in range(heads):
        o_ref[:, h * head : (h + 1) * head] = (acc_ref[h] / l_ref[h]).astype(BF)


def attention(own, img, kv, kvi, index, qpos, qstart, kpos, ownpos, ipos, iown):
    rows = own.shape[0]
    head = kv.shape[2] // 2
    heads = (own.shape[1] - 2 * head) // head
    return pl.pallas_call(
        attention_kernel,
        out_shape=jax.ShapeDtypeStruct((rows, heads * head), BF),
        scratch_shapes=[
            pltpu.VMEM((heads, rows, 1), F32),
            pltpu.VMEM((heads, rows, 1), F32),
            pltpu.VMEM((heads, rows, head), F32),
        ],
        compiler_params=pltpu.CompilerParams(vmem_limit_bytes=MEM),
        name="attention",
    )(own, img, kv, kvi, index, qpos, qstart, kpos, ownpos, ipos, iown)


def output_kernel(place_ref, att_ref, tok_ref, img_ref, index_ref, *refs):
    w_refs, (o_ref, buf_ref, sem_ref) = (refs[:-3], refs[-3:])
    step = pl.program_id(0)
    rows = tok_ref.shape[0]
    slots = img_ref.shape[0]
    tiles, _, lanes = buf_ref.shape[1:]
    index = index_ref[...]
    picker = (index == lax.broadcasted_iota(jnp.int32, (rows, slots), 1)).astype(F32).astype(BF)
    is_img = index < slots
    loads = piece_loads(w_refs, buf_ref, sem_ref)

    @pl.when(step == 0)
    def _():
        for load in loads:
            for copy in load:
                copy.start()

    for i, load in enumerate(loads):

        @pl.when(step == i)
        def _(load=load):
            for copy in load:
                copy.wait()

    for t in range(0, tiles, 2):
        at = slice(t * lanes, (t + 2) * lanes)
        w = jnp.concatenate([buf_ref[step, t], buf_ref[step, t + 1]], axis=1)
        update = dot_f32(att_ref[...], w)
        base = jnp.where(is_img, dot_f32(picker, img_ref[:, at]), tok_ref[:, at].astype(F32))
        o_ref[:, at] = (base + update).astype(BF)


def output_layer(place, att, tokens, images, index, parts):
    rows, width = tokens.shape
    slots = images.shape[0]
    tiles, depth, lanes = parts[0].shape
    cols = tiles * lanes
    column = lambda i, c: (0, c[i])
    return pl.pallas_call(
        output_kernel,
        grid_spec=pltpu.PrefetchScalarGridSpec(
            num_scalar_prefetch=1,
            grid=(8,),
            in_specs=[
                pl.BlockSpec(att.shape, lambda i, c: (0, 0)),
                pl.BlockSpec((rows, cols), column),
                pl.BlockSpec((slots, cols), column),
                pl.BlockSpec((rows, 1), lambda i, c: (0, 0)),
            ]
            + [pl.BlockSpec(memory_space=pl.ANY)] * len(parts),
            out_specs=pl.BlockSpec((rows, cols), column),
            scratch_shapes=[
                pltpu.VMEM((8, tiles, depth, lanes), BF),
                pltpu.SemaphoreType.DMA((len(parts),)),
            ],
        ),
        out_shape=jax.ShapeDtypeStruct((rows, width), BF),
        compiler_params=pltpu.CompilerParams(vmem_limit_bytes=MEM),
        name="output_layer",
    )(place, att, tokens, images, index, *parts)


def swap(x, axis):
    return lax.ppermute(x, axis, [(0, 1), (1, 0)])


def after(x, *others):
    return lax.optimization_barrier((x, *others))[0]


def in_order(mine, theirs, place, dim):
    return jnp.where(place == 0, jnp.stack([mine, theirs], dim), jnp.stack([theirs, mine], dim))


def along_x(x, steps):
    place = lambda at: (at % 2) * 2 + at // 2
    return lax.ppermute(x, (XLO, XHI), [(place(at), place((at + steps) % 4)) for at in range(4)])


def neighbours_x(x):
    return along_x(x, 1), along_x(x, 3)


def around_x(x, before, behind):
    half = x.shape[0] // 2
    return [x, before, behind, along_x(before[:half], 1), along_x(behind[half:], 3)]


def both_cores(parts, *held):
    return parts + [swap(after(part, *held), CORE) for part in parts]


def copies_to(x, axes):
    count = lax.axis_size(axes)
    return lax.all_to_all(jnp.broadcast_to(x[None], (count,) + x.shape), axes, 0, 0, tiled=True)


def half_across(x, axis, core):
    size = x.shape[axis] // 2
    return swap(lax.dynamic_slice_in_dim(x, core * size, size, axis), XHI)


def both_halves(mine, axis, core):
    size = mine.shape[axis]
    buffer = jnp.zeros(mine.shape[:axis] + (2 * size,) + mine.shape[axis + 1 :], mine.dtype)
    buffer = lax.dynamic_update_slice_in_dim(buffer, mine, core * size, axis)
    return lax.dynamic_update_slice_in_dim(buffer, swap(mine, CORE), (1 - core) * size, axis)


def keys_for_later(block, x_hi, zy):
    below = lax.ppermute(block, XHI, [(0, 1)])
    count = lax.axis_size(ZY)
    receiver = jnp.arange(count, dtype=jnp.int32)
    take_below = ((x_hi == 1) & (receiver <= zy)).reshape((count,) + (1,) * block.ndim)
    outgoing = jnp.where(take_below, below[None], block[None])
    return lax.all_to_all(outgoing, ZY, 0, 0, tiled=True)


def on_device(
    patches, piece_ids, vit_gain, vit_qkv, vit_out, merge_gain, merge_up, merge_down, dest,
    tokens, image_index, doc_lengths, attn_gain, attn_qkv, attn_out,
):
    core = lax.axis_index(CORE)
    x_hi = lax.axis_index(XHI)
    zy = lax.axis_index(ZY)
    y_odd = lax.axis_index(Y) % 2
    seq_count = lax.axis_size(SEQ)
    seq_index = lax.axis_index(SEQ)
    places = seq_count // 2
    tok_rows, width = tokens.shape

    depth, sliver = attn_out.shape
    upper, lower = (attn_out[: depth // 2], attn_out[depth // 2 :])
    give = jnp.where(y_odd == 1, upper, lower)
    keep = jnp.where(y_odd == 1, lower, upper)
    got = lax.ppermute(give, Y, [(0, 1), (1, 0), (2, 3), (3, 2)])
    tile = jnp.where(
        y_odd == 1, jnp.concatenate([got, keep], axis=1), jnp.concatenate([keep, got], axis=1)
    )
    spread = copies_to(after(attn_qkv, tile), ZY)
    qkv_piece = spread.reshape(-1, attn_qkv.shape[1])
    qkv_near = neighbours_x(qkv_piece)
    qkv_parts = around_x(qkv_piece, *qkv_near)
    chip_x = x_hi * 2 + lax.axis_index(XLO)
    place = [
        (source % 2) * 4 + side * 2 + source // 2
        for side in (core, 1 - core)
        for source in [(chip_x - steps) % 4 for steps in (0, 1, 3, 2)]
    ]
    place = jnp.stack(place).astype(jnp.int32)

    up_own = merge_up.T
    up_half = half_across(up_own, 1, core)
    down_half = half_across(after(merge_down, *qkv_near), 0, core)
    up_oth = both_halves(up_half, 1, core)
    down_oth = both_halves(down_half, 0, core)

    merge_in = window_layer(after(patches, up_half), piece_ids, vit_gain, vit_qkv, vit_out, merge_gain)
    own_rows = merge_in.shape[0]
    note = jnp.broadcast_to(dest.astype(BF)[:, None], (own_rows, 128))
    rows = copies_to(after(jnp.concatenate([merge_in, note], axis=1), spread), ZY)
    rows = rows.reshape(places * own_rows, -1)
    wide = merge_in.shape[1]
    out_spread = copies_to(after(tile, rows, *qkv_near), ZY)
    out_piece = after(out_spread.reshape(-1, depth, 2 * sliver), *qkv_parts[3:])
    out_near = neighbours_x(out_piece)
    out_parts = around_x(out_piece, *out_near)
    targets = rows[:, wide].astype(jnp.int32)

    def hidden(weights):
        total = dot_f32(weights, rows[:, :wide], 1, 1)
        return jax.nn.gelu(total, approximate=False).astype(BF)

    mine, theirs = (hidden(up_own), hidden(up_oth))
    pair = after(in_order(mine, theirs, x_hi, 0), out_spread)
    gathered = copies_to(pair, ZY)
    qkv_all = both_cores(qkv_parts, pair)

    proj_text = project(place, tokens, attn_gain, qkv_all)
    query_width = depth
    index_row = jnp.broadcast_to(image_index.astype(BF)[None, :], (16, tok_rows))
    block = jnp.concatenate([proj_text[:, query_width:], index_row], axis=0)
    block = after(block, gathered)
    kv_text = keys_for_later(block, x_hi, zy)
    hidden_0, hidden_1 = (gathered[:, i].reshape(-1, places * own_rows) for i in range(2))
    middle = hidden_0.shape[0]

    def columns(weights):
        return (
            dot_f32(hidden_0, weights[:middle], 0, 0) + dot_f32(hidden_1, weights[middle:], 0, 0)
        ).astype(BF)

    mine, theirs = (columns(merge_down), columns(down_oth))
    merged = jnp.concatenate(
        [jnp.where(x_hi == 0, mine, theirs), jnp.where(x_hi == 0, theirs, mine)], axis=1
    )

    receivers = jnp.arange(seq_count, dtype=jnp.int32)
    row_home = jnp.arange(places * own_rows, dtype=jnp.int32) // own_rows
    homes = jnp.arange(places, dtype=jnp.int32)
    select = (targets[None, None, :] == receivers[:, None, None]) & (
        row_home[None, None, :] == homes[None, :, None]
    )
    merged = after(merged, *out_near)
    outgoing = dot_f32(select.astype(BF).reshape(seq_count * places, -1), merged).astype(BF)
    arrived = lax.all_to_all(
        outgoing.reshape(seq_count, places, -1), SEQ, split_axis=0, concat_axis=0, tiled=True
    )
    arrived = arrived.reshape(2, places, places, 2, -1)
    images = arrived.transpose(0, 2, 3, 1, 4).reshape(seq_count, width)

    proj_img = project(place, after(images, *out_parts[3:]), attn_gain, qkv_all)
    kv_img = keys_for_later(proj_img[:, query_width:], x_hi, zy)

    positions = seq_index * tok_rows + jnp.arange(tok_rows, dtype=jnp.int32)
    lengths = doc_lengths[0]
    order_of = jnp.arange(lengths.shape[0], dtype=jnp.int32)
    starts = jnp.sum(jnp.where(order_of[None, :] < order_of[:, None], lengths[None, :], 0), axis=1)
    doc_start = jnp.max(jnp.where(starts[None, :] <= positions[:, None], starts[None, :], 0), axis=1)
    slot_ids = jnp.arange(seq_count, dtype=jnp.int32)
    within = jnp.arange(tok_rows, dtype=jnp.int32)
    home = jnp.where(x_hi == 0, homes, jnp.where(homes >= zy, homes, homes + places))
    useful = (x_hi == 1) | (homes < zy)
    indexes = kv_text[:, tok_rows, :].astype(jnp.int32)
    kpos = jnp.where(
        (indexes == seq_count) & useful[:, None], home[:, None] * tok_rows + within[None, :], FAR
    )
    ownpos = jnp.where(image_index == seq_count, positions, FAR)
    hits = indexes[:, None, :] == slot_ids[None, :, None]
    ipos = jnp.min(
        jnp.where(hits & useful[:, None, None], (home[:, None] * tok_rows + within[None, :])[:, None, :], FAR),
        axis=-1,
    )
    iown = jnp.min(
        jnp.where(image_index[None, :] == slot_ids[:, None], positions[None, :], FAR), axis=-1
    )

    out_all = both_cores(out_parts, proj_text)
    index_col = image_index.reshape(tok_rows, 1)
    attended = attention(
        proj_text,
        proj_img,
        kv_text,
        kv_img.reshape(-1, kv_img.shape[2]),
        index_col,
        positions.reshape(tok_rows, 1),
        doc_start.reshape(tok_rows, 1),
        kpos.reshape(places // 2, 1, 2 * tok_rows),
        ownpos.reshape(1, tok_rows),
        ipos.reshape(1, -1),
        iown.reshape(1, -1),
    )
    return output_layer(place, attended, tokens, images, index_col, out_all)


def solution(mesh):
    torus = Mesh(mesh.devices.reshape(2, 2, 2, 4, 4), GRP_SEQ)
    return jax.shard_map(
        on_device,
        mesh=torus,
        in_specs=(
            P(GRP_SEQ, None),
            P(GRP_SEQ, None),
            P(),
            P(),
            P(),
            P(),
            P(None, SEQ),
            P(None, SEQ),
            P(GRP_SEQ),
            P(GRP_SEQ, None),
            P(GRP_SEQ),
            P(GRP, None),
            P(),
            P(GRP_SEQ, None),
            P(None, GRP_SEQ),
        ),
        out_specs=P(GRP_SEQ, None),
        check_vma=False,
    )
```

```python
import jax
import jax.numpy as jnp
from jax import lax
from jax.experimental import pallas as pl
from jax.experimental.pallas import tpu as pltpu
from jax.sharding import Mesh
from jax.sharding import PartitionSpec as P

VHEADS = 16
XLO, CORE, XHI, Z, Y = ("grp_0", "grp_1", "seq_0", "seq_1", "seq_2")
SEQ = (XHI, Z, Y)
ZY = (Z, Y)
GRP_SEQ = (XLO, CORE, XHI, Z, Y)
GRP = (XLO, CORE)
EPSILON = 1e-06
NEG = -1e30
FAR = 1 << 30
BF = jnp.bfloat16
F32 = jnp.float32
MEM = 56 * 1024 * 1024


def dot_f32(a, b, ca=1, cb=0):
    return lax.dot_general(a, b, (((ca,), (cb,)), ((), ())), preferred_element_type=F32)


def window_kernel(x_ref, prow_ref, pcol_ref, gain_ref, w_ref, wo_ref, mgain_ref, o_ref, n_ref, p_ref):
    step = pl.program_id(0)
    rows, feats = x_ref.shape
    head = feats // VHEADS

    @pl.when(step == 0)
    def _():
        x = x_ref[...].astype(F32)
        mean = jnp.mean(x * x, axis=-1, keepdims=True)
        n_ref[...] = (x * lax.rsqrt(mean + EPSILON) * gain_ref[...]).astype(BF)

    for part in range(3):

        @pl.when(step == part)
        def _(part=part):
            p_ref[part] = dot_f32(n_ref[...], w_ref[...]).astype(BF)

    @pl.when(step == 2)
    def _():
        q, k, v = (p_ref[0], p_ref[1], p_ref[2])
        lane = lax.broadcasted_iota(jnp.int32, (rows, feats), 1)
        same = pcol_ref[...] == prow_ref[...]
        mixed = jnp.zeros((rows, feats), F32)
        for h in range(VHEADS):
            mine = (lane >= h * head) & (lane < (h + 1) * head)
            s = dot_f32(jnp.where(mine, q, jnp.zeros_like(q)), k, 1, 1) * head ** (-0.5)
            s = jnp.where(same, s, NEG)
            w = jnp.exp(s - jnp.max(s, axis=-1, keepdims=True))
            total = jnp.sum(w, axis=-1, keepdims=True)
            mixed = jnp.where(mine, dot_f32(w.astype(BF), v) / total, mixed)
        resid = x_ref[...].astype(F32) + dot_f32(mixed.astype(BF), wo_ref[...])
        mean = jnp.mean(resid * resid, axis=-1, keepdims=True)
        merged = (resid * lax.rsqrt(mean + EPSILON) * mgain_ref[...]).astype(BF)
        r_out = lax.broadcasted_iota(jnp.int32, (rows // 4, rows), 0)
        r_in = lax.broadcasted_iota(jnp.int32, (rows // 4, rows), 1)
        for j in range(4):
            pick = jnp.where(r_in == 4 * r_out + j, 1.0, 0.0).astype(BF)
            o_ref[:, j * feats : (j + 1) * feats] = dot_f32(pick, merged).astype(BF)


def window_layer(patches, piece_ids, vit_gain, vit_qkv, vit_out, merge_gain):
    rows, feats = patches.shape
    whole = lambda *shape: pl.BlockSpec(shape, lambda i: (0,) * len(shape))
    return pl.pallas_call(
        window_kernel,
        grid=(3,),
        in_specs=[
            whole(rows, feats),
            whole(1, rows),
            whole(rows, 1),
            whole(1, feats),
            pl.BlockSpec((feats, feats), lambda i: (0, i)),
            whole(feats, feats),
            whole(1, feats),
        ],
        out_specs=whole(rows // 4, 4 * feats),
        out_shape=jax.ShapeDtypeStruct((rows // 4, 4 * feats), BF),
        scratch_shapes=[pltpu.VMEM((rows, feats), BF), pltpu.VMEM((3, rows, feats), BF)],
        compiler_params=pltpu.CompilerParams(vmem_limit_bytes=MEM),
        name="window_layer",
    )(
        patches,
        piece_ids.reshape(1, rows),
        piece_ids.reshape(rows, 1),
        vit_gain.reshape(1, feats),
        vit_qkv,
        vit_out,
        merge_gain.reshape(1, feats),
    )


def piece_loads(refs, buf_ref, sem_ref):
    half = buf_ref.shape[1] // 2
    loads = []
    for side in range(2):
        own = refs[side * 5 : side * 5 + 5]
        for k in range(4):
            slot = side * 4 + k
            if k < 3:
                spots = [(own[k], buf_ref.at[slot])]
            else:
                spots = [(own[3 + i], buf_ref.at[slot, pl.ds(i * half, half)]) for i in range(2)]
            loads.append(
                [pltpu.make_async_copy(w, spot, sem_ref.at[side * 5 + k + i]) for i, (w, spot) in enumerate(spots)]
            )
    return loads


def project_kernel(place_ref, x_ref, gain_ref, *refs):
    w_refs, (o_ref, buf_ref, sem_ref) = (refs[:-3], refs[-3:])
    rows, width = x_ref.shape
    depth = buf_ref.shape[1]
    loads = piece_loads(w_refs, buf_ref, sem_ref)
    for load in loads:
        for copy in load:
            copy.start()
    total = jnp.zeros((rows, 1), F32)
    for c in range(0, width, depth):
        x = x_ref[:, c : c + depth].astype(F32)
        total = total + jnp.sum(x * x, axis=-1, keepdims=True)
    scale = lax.rsqrt(total / width + EPSILON)
    acc = jnp.zeros(o_ref.shape, F32)
    for i, load in enumerate(loads):
        start = pl.multiple_of(place_ref[i] * depth, depth)
        x = x_ref[:, pl.ds(start, depth)].astype(F32)
        n = (x * scale * gain_ref[:, pl.ds(start, depth)]).astype(BF)
        for copy in load:
            copy.wait()
        acc = acc + dot_f32(n, buf_ref[i])
    o_ref[...] = acc.astype(BF)


def project(place, x, gain, parts):
    rows, width = x.shape
    depth, cols = parts[0].shape
    return pl.pallas_call(
        project_kernel,
        grid_spec=pltpu.PrefetchScalarGridSpec(
            num_scalar_prefetch=1,
            grid=(1,),
            in_specs=[
                pl.BlockSpec((rows, width), lambda i, c: (0, 0)),
                pl.BlockSpec((1, width), lambda i, c: (0, 0)),
            ]
            + [pl.BlockSpec(memory_space=pl.ANY)] * len(parts),
            out_specs=pl.BlockSpec((rows, cols), lambda i, c: (0, 0)),
            scratch_shapes=[
                pltpu.VMEM((8, depth, cols), BF),
                pltpu.SemaphoreType.DMA((len(parts),)),
            ],
        ),
        out_shape=jax.ShapeDtypeStruct((rows, cols), BF),
        compiler_params=pltpu.CompilerParams(vmem_limit_bytes=MEM),
        name="project",
    )(place, x, gain.reshape(1, width), *parts)


def fold_keys(query, keys, values, allowed, h, scale, m_ref, l_ref, acc_ref):
    s = jnp.where(allowed, dot_f32(query, keys, 1, 1) * scale, NEG)
    old = m_ref[h]
    new = jnp.maximum(old, jnp.max(s, axis=-1, keepdims=True))
    shrink = jnp.exp(old - new)
    w = jnp.exp(s - new)
    l_ref[h] = l_ref[h] * shrink + jnp.sum(w, axis=-1, keepdims=True)
    acc_ref[h] = acc_ref[h] * shrink + dot_f32(w.astype(BF), values)
    m_ref[h] = new


def text_kernel(
    own_ref, img_ref, kv_ref, index_ref, qpos_ref, qstart_ref, kpos_ref, ownpos_ref,
    q_ref, m_ref, l_ref, acc_ref,
):
    rows = own_ref.shape[0]
    slots = img_ref.shape[0]
    head = kv_ref.shape[2] // 2
    width = q_ref.shape[1]
    heads = width // head
    blocks = kv_ref.shape[0]
    m_ref[...] = jnp.full_like(m_ref, NEG)
    l_ref[...] = jnp.zeros_like(l_ref)
    acc_ref[...] = jnp.zeros_like(acc_ref)
    index = index_ref[...]
    picker = (index == lax.broadcasted_iota(jnp.int32, (rows, slots), 1)).astype(F32).astype(BF)
    q_ref[...] = jnp.where(
        index < slots, dot_f32(picker, img_ref[:, :width]), own_ref[:, :width].astype(F32)
    ).astype(BF)
    qpos, qstart = (qpos_ref[...], qstart_ref[...])

    def fold(keys, values, kpos):
        allowed = (kpos >= qstart) & (kpos <= qpos)
        for h in range(heads):
            query = q_ref[:, h * head : (h + 1) * head]
            fold_keys(query, keys, values, allowed, h, head ** (-0.5), m_ref, l_ref, acc_ref)

    fold(own_ref[:, width : width + head], own_ref[:, width + head :], ownpos_ref[...])

    def step(i, carry):
        pair = kv_ref[pl.ds(2 * i, 2), :rows, :].reshape(2 * rows, 2 * head)
        fold(pair[:, :head], pair[:, head:], kpos_ref[i])
        return carry

    lax.fori_loop(0, blocks // 2, step, 0)


def text_attention(own, img, kv, index, qpos, qstart, kpos, ownpos):
    rows = own.shape[0]
    head = kv.shape[2] // 2
    heads = (own.shape[1] - 2 * head) // head
    return pl.pallas_call(
        text_kernel,
        out_shape=(
            jax.ShapeDtypeStruct((rows, heads * head), BF),
            jax.ShapeDtypeStruct((heads, rows, 1), F32),
            jax.ShapeDtypeStruct((heads, rows, 1), F32),
            jax.ShapeDtypeStruct((heads, rows, head), F32),
        ),
        compiler_params=pltpu.CompilerParams(vmem_limit_bytes=MEM),
        name="text_attention",
    )(own, img, kv, index, qpos, qstart, kpos, ownpos)


def image_kernel(
    q_ref, m_in, l_in, acc_in, img_ref, kvi_ref, qpos_ref, qstart_ref, ipos_ref, iown_ref,
    o_ref, m_ref, l_ref, acc_ref,
):
    head = acc_in.shape[2]
    heads = acc_in.shape[0]
    width = heads * head
    m_ref[...] = m_in[...]
    l_ref[...] = l_in[...]
    acc_ref[...] = acc_in[...]
    qpos, qstart = (qpos_ref[...], qstart_ref[...])
    for keys, values, kpos in (
        (kvi_ref[:, :head], kvi_ref[:, head:], ipos_ref[...]),
        (img_ref[:, width : width + head], img_ref[:, width + head :], iown_ref[...]),
    ):
        allowed = (kpos >= qstart) & (kpos <= qpos)
        for h in range(heads):
            query = q_ref[:, h * head : (h + 1) * head]
            fold_keys(query, keys, values, allowed, h, head ** (-0.5), m_ref, l_ref, acc_ref)
    for h in range(heads):
        o_ref[:, h * head : (h + 1) * head] = (acc_ref[h] / l_ref[h]).astype(BF)


def image_attention(q, m, l, acc, img, kvi, qpos, qstart, ipos, iown):
    return pl.pallas_call(
        image_kernel,
        out_shape=jax.ShapeDtypeStruct(q.shape, BF),
        scratch_shapes=[pltpu.VMEM(m.shape, F32), pltpu.VMEM(l.shape, F32), pltpu.VMEM(acc.shape, F32)],
        compiler_params=pltpu.CompilerParams(vmem_limit_bytes=MEM),
        name="image_attention",
    )(q, m, l, acc, img, kvi, qpos, qstart, ipos, iown)


def layer_kernel(tok_ref, img_ref, index_ref, o_ref):
    rows, cols = tok_ref.shape
    slots = img_ref.shape[0]
    index = index_ref[...]
    picker = (index == lax.broadcasted_iota(jnp.int32, (rows, slots), 1)).astype(F32).astype(BF)
    picked = dot_f32(picker, img_ref[...])
    o_ref[...] = jnp.where(index < slots, picked, tok_ref[...].astype(F32)).astype(BF)


def layer_input(tokens, images, index):
    rows, width = tokens.shape
    cols = width // 4
    return pl.pallas_call(
        layer_kernel,
        grid=(4,),
        in_specs=[
            pl.BlockSpec((rows, cols), lambda i: (0, i)),
            pl.BlockSpec((images.shape[0], cols), lambda i: (0, i)),
            pl.BlockSpec((rows, 1), lambda i: (0, 0)),
        ],
        out_specs=pl.BlockSpec((rows, cols), lambda i: (0, i)),
        out_shape=jax.ShapeDtypeStruct((rows, width), BF),
        compiler_params=pltpu.CompilerParams(vmem_limit_bytes=MEM),
        name="layer_input",
    )(tokens, images, index)


def output_kernel(place_ref, att_ref, in_ref, *refs):
    w_refs, (o_ref, buf_ref, sem_ref) = (refs[:-3], refs[-3:])
    step = pl.program_id(0)
    tiles, _, lanes = buf_ref.shape[1:]
    loads = piece_loads(w_refs, buf_ref, sem_ref)

    @pl.when(step == 0)
    def _():
        for load in loads:
            for copy in load:
                copy.start()

    for i, load in enumerate(loads):

        @pl.when(step == i)
        def _(load=load):
            for copy in load:
                copy.wait()

    for t in range(0, tiles, 2):
        at = slice(t * lanes, (t + 2) * lanes)
        w = jnp.concatenate([buf_ref[step, t], buf_ref[step, t + 1]], axis=1)
        o_ref[:, at] = (in_ref[:, at].astype(F32) + dot_f32(att_ref[...], w)).astype(BF)


def output_layer(place, att, layer_in, parts):
    rows, width = layer_in.shape
    tiles, depth, lanes = parts[0].shape
    column = lambda i, c: (0, c[i])
    return pl.pallas_call(
        output_kernel,
        grid_spec=pltpu.PrefetchScalarGridSpec(
            num_scalar_prefetch=1,
            grid=(8,),
            in_specs=[
                pl.BlockSpec(att.shape, lambda i, c: (0, 0)),
                pl.BlockSpec((rows, tiles * lanes), column),
            ]
            + [pl.BlockSpec(memory_space=pl.ANY)] * len(parts),
            out_specs=pl.BlockSpec((rows, tiles * lanes), column),
            scratch_shapes=[
                pltpu.VMEM((8, tiles, depth, lanes), BF),
                pltpu.SemaphoreType.DMA((len(parts),)),
            ],
        ),
        out_shape=jax.ShapeDtypeStruct((rows, width), BF),
        compiler_params=pltpu.CompilerParams(vmem_limit_bytes=MEM),
        name="output_layer",
    )(place, att, layer_in, *parts)


def swap(x, axis):
    return lax.ppermute(x, axis, [(0, 1), (1, 0)])


def after(x, *others):
    return lax.optimization_barrier((x, *others))[0]


def in_order(mine, theirs, place, dim):
    return jnp.where(place == 0, jnp.stack([mine, theirs], dim), jnp.stack([theirs, mine], dim))


def along_x(x, steps):
    place = lambda at: (at % 2) * 2 + at // 2
    return lax.ppermute(x, (XLO, XHI), [(place(at), place((at + steps) % 4)) for at in range(4)])


def neighbours_x(x):
    return along_x(x, 1), along_x(x, 3)


def around_x(x, before, behind):
    half = x.shape[0] // 2
    return [x, before, behind, along_x(before[:half], 1), along_x(behind[half:], 3)]


def both_cores(parts, *held):
    return parts + [swap(after(part, *held), CORE) for part in parts]


def copies_to(x, axes):
    count = lax.axis_size(axes)
    return lax.all_to_all(jnp.broadcast_to(x[None], (count,) + x.shape), axes, 0, 0, tiled=True)


def half_across(x, axis, core):
    size = x.shape[axis] // 2
    return swap(lax.dynamic_slice_in_dim(x, core * size, size, axis), XHI)


def both_halves(mine, axis, core):
    size = mine.shape[axis]
    buffer = jnp.zeros(mine.shape[:axis] + (2 * size,) + mine.shape[axis + 1 :], mine.dtype)
    buffer = lax.dynamic_update_slice_in_dim(buffer, mine, core * size, axis)
    return lax.dynamic_update_slice_in_dim(buffer, swap(mine, CORE), (1 - core) * size, axis)


def keys_for_later(block, x_hi, zy):
    below = lax.ppermute(block, XHI, [(0, 1)])
    count = lax.axis_size(ZY)
    receiver = jnp.arange(count, dtype=jnp.int32)
    take_below = ((x_hi == 1) & (receiver <= zy)).reshape((count,) + (1,) * block.ndim)
    outgoing = jnp.where(take_below, below[None], block[None])
    return lax.all_to_all(outgoing, ZY, 0, 0, tiled=True)


def on_device(
    patches, piece_ids, vit_gain, vit_qkv, vit_out, merge_gain, merge_up, merge_down, dest,
    tokens, image_index, doc_lengths, attn_gain, attn_qkv, attn_out,
):
    core = lax.axis_index(CORE)
    x_hi = lax.axis_index(XHI)
    zy = lax.axis_index(ZY)
    y_odd = lax.axis_index(Y) % 2
    seq_count = lax.axis_size(SEQ)
    seq_index = lax.axis_index(SEQ)
    places = seq_count // 2
    tok_rows, width = tokens.shape

    depth, sliver = attn_out.shape
    upper, lower = (attn_out[: depth // 2], attn_out[depth // 2 :])
    give = jnp.where(y_odd == 1, upper, lower)
    keep = jnp.where(y_odd == 1, lower, upper)
    got = lax.ppermute(give, Y, [(0, 1), (1, 0), (2, 3), (3, 2)])
    tile = jnp.where(
        y_odd == 1, jnp.concatenate([got, keep], axis=1), jnp.concatenate([keep, got], axis=1)
    )
    spread = copies_to(after(attn_qkv, tile), ZY)
    qkv_piece = spread.reshape(-1, attn_qkv.shape[1])
    qkv_near = neighbours_x(qkv_piece)
    qkv_parts = around_x(qkv_piece, *qkv_near)
    chip_x = x_hi * 2 + lax.axis_index(XLO)
    place = [
        (source % 2) * 4 + side * 2 + source // 2
        for side in (core, 1 - core)
        for source in [(chip_x - steps) % 4 for steps in (0, 1, 3, 2)]
    ]
    place = jnp.stack(place).astype(jnp.int32)

    up_own = merge_up.T
    up_half = half_across(up_own, 1, core)
    down_half = half_across(after(merge_down, *qkv_near), 0, core)
    up_oth = both_halves(up_half, 1, core)
    down_oth = both_halves(down_half, 0, core)

    merge_in = window_layer(after(patches, up_half), piece_ids, vit_gain, vit_qkv, vit_out, merge_gain)
    own_rows = merge_in.shape[0]
    note = jnp.broadcast_to(dest.astype(BF)[:, None], (own_rows, 128))
    rows = copies_to(after(jnp.concatenate([merge_in, note], axis=1), spread), ZY)
    rows = rows.reshape(places * own_rows, -1)
    wide = merge_in.shape[1]
    out_spread = copies_to(after(tile, rows, *qkv_near), ZY)
    out_piece = after(out_spread.reshape(-1, depth, 2 * sliver), *qkv_parts[3:])
    out_near = neighbours_x(out_piece)
    out_parts = around_x(out_piece, *out_near)
    targets = rows[:, wide].astype(jnp.int32)

    def hidden(weights):
        total = dot_f32(weights, rows[:, :wide], 1, 1)
        return jax.nn.gelu(total, approximate=False).astype(BF)

    mine, theirs = (hidden(up_own), hidden(up_oth))
    pair = after(in_order(mine, theirs, x_hi, 0), out_spread)
    gathered = copies_to(pair, ZY)
    qkv_all = both_cores(qkv_parts, pair)

    hidden_0, hidden_1 = (gathered[:, i].reshape(-1, places * own_rows) for i in range(2))
    middle = hidden_0.shape[0]

    def columns(weights):
        return (
            dot_f32(hidden_0, weights[:middle], 0, 0) + dot_f32(hidden_1, weights[middle:], 0, 0)
        ).astype(BF)

    mine, theirs = (columns(merge_down), columns(down_oth))
    merged = jnp.concatenate(
        [jnp.where(x_hi == 0, mine, theirs), jnp.where(x_hi == 0, theirs, mine)], axis=1
    )

    receivers = jnp.arange(seq_count, dtype=jnp.int32)
    row_home = jnp.arange(places * own_rows, dtype=jnp.int32) // own_rows
    homes = jnp.arange(places, dtype=jnp.int32)
    select = (targets[None, None, :] == receivers[:, None, None]) & (
        row_home[None, None, :] == homes[None, :, None]
    )
    outgoing = dot_f32(select.astype(BF).reshape(seq_count * places, -1), merged).astype(BF)
    proj_text = project(place, after(tokens, outgoing), attn_gain, qkv_all)
    query_width = depth
    index_row = jnp.broadcast_to(image_index.astype(BF)[None, :], (16, tok_rows))
    block = jnp.concatenate([proj_text[:, query_width:], index_row], axis=0)
    block = after(block, *out_near)
    kv_text = keys_for_later(block, x_hi, zy)
    arrived = lax.all_to_all(
        outgoing.reshape(seq_count, places, -1), SEQ, split_axis=0, concat_axis=0, tiled=True
    )
    arrived = arrived.reshape(2, places, places, 2, -1)
    images = arrived.transpose(0, 2, 3, 1, 4).reshape(seq_count, width)

    proj_img = project(place, after(images, *out_parts[3:]), attn_gain, qkv_all)
    kv_img = keys_for_later(proj_img[:, query_width:], x_hi, zy)

    positions = seq_index * tok_rows + jnp.arange(tok_rows, dtype=jnp.int32)
    lengths = doc_lengths[0]
    order_of = jnp.arange(lengths.shape[0], dtype=jnp.int32)
    starts = jnp.sum(jnp.where(order_of[None, :] < order_of[:, None], lengths[None, :], 0), axis=1)
    doc_start = jnp.max(jnp.where(starts[None, :] <= positions[:, None], starts[None, :], 0), axis=1)
    slot_ids = jnp.arange(seq_count, dtype=jnp.int32)
    within = jnp.arange(tok_rows, dtype=jnp.int32)
    home = jnp.where(x_hi == 0, homes, jnp.where(homes >= zy, homes, homes + places))
    useful = (x_hi == 1) | (homes < zy)
    indexes = kv_text[:, tok_rows, :].astype(jnp.int32)
    kpos = jnp.where(
        (indexes == seq_count) & useful[:, None], home[:, None] * tok_rows + within[None, :], FAR
    )
    ownpos = jnp.where(image_index == seq_count, positions, FAR)
    hits = indexes[:, None, :] == slot_ids[None, :, None]
    ipos = jnp.min(
        jnp.where(hits & useful[:, None, None], (home[:, None] * tok_rows + within[None, :])[:, None, :], FAR),
        axis=-1,
    )
    iown = jnp.min(
        jnp.where(image_index[None, :] == slot_ids[:, None], positions[None, :], FAR), axis=-1
    )

    out_all = both_cores(out_parts, proj_text)
    index_col = image_index.reshape(tok_rows, 1)
    qpos, qstart = (positions.reshape(tok_rows, 1), doc_start.reshape(tok_rows, 1))
    query, high, total, mixed = text_attention(
        proj_text, proj_img, kv_text, index_col, qpos, qstart,
        kpos.reshape(places // 2, 1, 2 * tok_rows), ownpos.reshape(1, tok_rows),
    )
    layer_in = layer_input(tokens, images, after(index_col, proj_img))
    attended = image_attention(
        query, high, total, mixed, proj_img, kv_img.reshape(-1, kv_img.shape[2]),
        qpos, qstart, ipos.reshape(1, -1), iown.reshape(1, -1),
    )
    return output_layer(place, attended, layer_in, out_all)


def solution(mesh):
    torus = Mesh(mesh.devices.reshape(2, 2, 2, 4, 4), GRP_SEQ)
    return jax.shard_map(
        on_device,
        mesh=torus,
        in_specs=(
            P(GRP_SEQ, None),
            P(GRP_SEQ, None),
            P(),
            P(),
            P(),
            P(),
            P(None, SEQ),
            P(None, SEQ),
            P(GRP_SEQ),
            P(GRP_SEQ, None),
            P(GRP_SEQ),
            P(GRP, None),
            P(),
            P(GRP_SEQ, None),
            P(None, GRP_SEQ),
        ),
        out_specs=P(GRP_SEQ, None),
        check_vma=False,
    )
```

```python
import jax
import jax.numpy as jnp
from jax import lax
from jax.experimental import pallas as pl
from jax.experimental.pallas import tpu as pltpu
from jax.sharding import Mesh
from jax.sharding import PartitionSpec as P

VHEADS = 16
XLO, CORE, XHI, Z, Y = ("grp_0", "grp_1", "seq_0", "seq_1", "seq_2")
SEQ = (XHI, Z, Y)
ZY = (Z, Y)
GRP_SEQ = (XLO, CORE, XHI, Z, Y)
GRP = (XLO, CORE)
EPSILON = 1e-06
NEG = -1e30
FAR = 1 << 30
BF = jnp.bfloat16
F32 = jnp.float32
MEM = 56 * 1024 * 1024


def dot_f32(a, b, ca=1, cb=0):
    return lax.dot_general(a, b, (((ca,), (cb,)), ((), ())), preferred_element_type=F32)


def window_kernel(x_ref, prow_ref, pcol_ref, gain_ref, w_ref, wo_ref, mgain_ref, o_ref, n_ref, p_ref):
    step = pl.program_id(0)
    rows, feats = x_ref.shape
    head = feats // VHEADS

    @pl.when(step == 0)
    def _():
        x = x_ref[...].astype(F32)
        mean = jnp.mean(x * x, axis=-1, keepdims=True)
        n_ref[...] = (x * lax.rsqrt(mean + EPSILON) * gain_ref[...]).astype(BF)

    for part in range(3):

        @pl.when(step == part)
        def _(part=part):
            p_ref[part] = dot_f32(n_ref[...], w_ref[...]).astype(BF)

    @pl.when(step == 2)
    def _():
        q, k, v = (p_ref[0], p_ref[1], p_ref[2])
        lane = lax.broadcasted_iota(jnp.int32, (rows, feats), 1)
        same = pcol_ref[...] == prow_ref[...]
        mixed = jnp.zeros((rows, feats), F32)
        for h in range(VHEADS):
            mine = (lane >= h * head) & (lane < (h + 1) * head)
            s = dot_f32(jnp.where(mine, q, jnp.zeros_like(q)), k, 1, 1) * head ** (-0.5)
            s = jnp.where(same, s, NEG)
            w = jnp.exp(s - jnp.max(s, axis=-1, keepdims=True))
            total = jnp.sum(w, axis=-1, keepdims=True)
            mixed = jnp.where(mine, dot_f32(w.astype(BF), v) / total, mixed)
        resid = x_ref[...].astype(F32) + dot_f32(mixed.astype(BF), wo_ref[...])
        mean = jnp.mean(resid * resid, axis=-1, keepdims=True)
        merged = (resid * lax.rsqrt(mean + EPSILON) * mgain_ref[...]).astype(BF)
        r_out = lax.broadcasted_iota(jnp.int32, (rows // 4, rows), 0)
        r_in = lax.broadcasted_iota(jnp.int32, (rows // 4, rows), 1)
        for j in range(4):
            pick = jnp.where(r_in == 4 * r_out + j, 1.0, 0.0).astype(BF)
            o_ref[:, j * feats : (j + 1) * feats] = dot_f32(pick, merged).astype(BF)


def window_layer(patches, piece_ids, vit_gain, vit_qkv, vit_out, merge_gain):
    rows, feats = patches.shape
    whole = lambda *shape: pl.BlockSpec(shape, lambda i: (0,) * len(shape))
    return pl.pallas_call(
        window_kernel,
        grid=(3,),
        in_specs=[
            whole(rows, feats),
            whole(1, rows),
            whole(rows, 1),
            whole(1, feats),
            pl.BlockSpec((feats, feats), lambda i: (0, i)),
            whole(feats, feats),
            whole(1, feats),
        ],
        out_specs=whole(rows // 4, 4 * feats),
        out_shape=jax.ShapeDtypeStruct((rows // 4, 4 * feats), BF),
        scratch_shapes=[pltpu.VMEM((rows, feats), BF), pltpu.VMEM((3, rows, feats), BF)],
        compiler_params=pltpu.CompilerParams(vmem_limit_bytes=MEM),
        name="window_layer",
    )(
        patches,
        piece_ids.reshape(1, rows),
        piece_ids.reshape(rows, 1),
        vit_gain.reshape(1, feats),
        vit_qkv,
        vit_out,
        merge_gain.reshape(1, feats),
    )


def piece_loads(refs, buf_ref, sem_ref):
    half = buf_ref.shape[1] // 2
    loads = []
    for side in range(2):
        own = refs[side * 5 : side * 5 + 5]
        for k in range(4):
            slot = side * 4 + k
            if k < 3:
                spots = [(own[k], buf_ref.at[slot])]
            else:
                spots = [(own[3 + i], buf_ref.at[slot, pl.ds(i * half, half)]) for i in range(2)]
            loads.append(
                [pltpu.make_async_copy(w, spot, sem_ref.at[side * 5 + k + i]) for i, (w, spot) in enumerate(spots)]
            )
    return loads


def project_kernel(place_ref, x_ref, gain_ref, *refs):
    w_refs, (o_ref, buf_ref, sem_ref) = (refs[:-3], refs[-3:])
    rows, width = x_ref.shape
    depth = buf_ref.shape[1]
    loads = piece_loads(w_refs, buf_ref, sem_ref)
    for load in loads:
        for copy in load:
            copy.start()
    total = jnp.zeros((rows, 1), F32)
    for c in range(0, width, depth):
        x = x_ref[:, c : c + depth].astype(F32)
        total = total + jnp.sum(x * x, axis=-1, keepdims=True)
    scale = lax.rsqrt(total / width + EPSILON)
    acc = jnp.zeros(o_ref.shape, F32)
    for i, load in enumerate(loads):
        start = pl.multiple_of(place_ref[i] * depth, depth)
        x = x_ref[:, pl.ds(start, depth)].astype(F32)
        n = (x * scale * gain_ref[:, pl.ds(start, depth)]).astype(BF)
        for copy in load:
            copy.wait()
        acc = acc + dot_f32(n, buf_ref[i])
    o_ref[...] = acc.astype(BF)


def project(place, x, gain, parts):
    rows, width = x.shape
    depth, cols = parts[0].shape
    return pl.pallas_call(
        project_kernel,
        grid_spec=pltpu.PrefetchScalarGridSpec(
            num_scalar_prefetch=1,
            grid=(1,),
            in_specs=[
                pl.BlockSpec((rows, width), lambda i, c: (0, 0)),
                pl.BlockSpec((1, width), lambda i, c: (0, 0)),
            ]
            + [pl.BlockSpec(memory_space=pl.ANY)] * len(parts),
            out_specs=pl.BlockSpec((rows, cols), lambda i, c: (0, 0)),
            scratch_shapes=[
                pltpu.VMEM((8, depth, cols), BF),
                pltpu.SemaphoreType.DMA((len(parts),)),
            ],
        ),
        out_shape=jax.ShapeDtypeStruct((rows, cols), BF),
        compiler_params=pltpu.CompilerParams(vmem_limit_bytes=MEM),
        name="project",
    )(place, x, gain.reshape(1, width), *parts)


def fold_keys(query, keys, values, allowed, h, scale, m_ref, l_ref, acc_ref):
    s = jnp.where(allowed, dot_f32(query, keys, 1, 1) * scale, NEG)
    old = m_ref[h]
    new = jnp.maximum(old, jnp.max(s, axis=-1, keepdims=True))
    shrink = jnp.exp(old - new)
    w = jnp.exp(s - new)
    l_ref[h] = l_ref[h] * shrink + jnp.sum(w, axis=-1, keepdims=True)
    acc_ref[h] = acc_ref[h] * shrink + dot_f32(w.astype(BF), values)
    m_ref[h] = new


def text_kernel(
    own_ref, img_ref, kv_ref, index_ref, qpos_ref, qstart_ref, kpos_ref, ownpos_ref,
    q_ref, m_ref, l_ref, acc_ref,
):
    rows = own_ref.shape[0]
    slots = img_ref.shape[0]
    head = kv_ref.shape[2] // 2
    width = q_ref.shape[1]
    heads = width // head
    blocks = kv_ref.shape[0]
    m_ref[...] = jnp.full_like(m_ref, NEG)
    l_ref[...] = jnp.zeros_like(l_ref)
    acc_ref[...] = jnp.zeros_like(acc_ref)
    index = index_ref[...]
    picker = (index == lax.broadcasted_iota(jnp.int32, (rows, slots), 1)).astype(F32).astype(BF)
    q_ref[...] = jnp.where(
        index < slots, dot_f32(picker, img_ref[:, :width]), own_ref[:, :width].astype(F32)
    ).astype(BF)
    qpos, qstart = (qpos_ref[...], qstart_ref[...])

    def fold(keys, values, kpos):
        allowed = (kpos >= qstart) & (kpos <= qpos)
        for h in range(heads):
            query = q_ref[:, h * head : (h + 1) * head]
            fold_keys(query, keys, values, allowed, h, head ** (-0.5), m_ref, l_ref, acc_ref)

    fold(own_ref[:, width : width + head], own_ref[:, width + head :], ownpos_ref[...])

    def step(i, carry):
        pair = kv_ref[pl.ds(2 * i, 2), :rows, :].reshape(2 * rows, 2 * head)
        fold(pair[:, :head], pair[:, head:], kpos_ref[i])
        return carry

    lax.fori_loop(0, blocks // 2, step, 0)


def text_attention(own, img, kv, index, qpos, qstart, kpos, ownpos):
    rows = own.shape[0]
    head = kv.shape[2] // 2
    heads = (own.shape[1] - 2 * head) // head
    return pl.pallas_call(
        text_kernel,
        out_shape=(
            jax.ShapeDtypeStruct((rows, heads * head), BF),
            jax.ShapeDtypeStruct((heads, rows, 1), F32),
            jax.ShapeDtypeStruct((heads, rows, 1), F32),
            jax.ShapeDtypeStruct((heads, rows, head), F32),
        ),
        compiler_params=pltpu.CompilerParams(vmem_limit_bytes=MEM),
        name="text_attention",
    )(own, img, kv, index, qpos, qstart, kpos, ownpos)


def image_kernel(
    q_ref, m_in, l_in, acc_in, img_ref, kvi_ref, qpos_ref, qstart_ref, ipos_ref, iown_ref,
    o_ref, m_ref, l_ref, acc_ref,
):
    head = acc_in.shape[2]
    heads = acc_in.shape[0]
    width = heads * head
    m_ref[...] = m_in[...]
    l_ref[...] = l_in[...]
    acc_ref[...] = acc_in[...]
    qpos, qstart = (qpos_ref[...], qstart_ref[...])
    for keys, values, kpos in (
        (kvi_ref[:, :head], kvi_ref[:, head:], ipos_ref[...]),
        (img_ref[:, width : width + head], img_ref[:, width + head :], iown_ref[...]),
    ):
        allowed = (kpos >= qstart) & (kpos <= qpos)
        for h in range(heads):
            query = q_ref[:, h * head : (h + 1) * head]
            fold_keys(query, keys, values, allowed, h, head ** (-0.5), m_ref, l_ref, acc_ref)
    for h in range(heads):
        o_ref[:, h * head : (h + 1) * head] = (acc_ref[h] / l_ref[h]).astype(BF)


def image_attention(q, m, l, acc, img, kvi, qpos, qstart, ipos, iown):
    return pl.pallas_call(
        image_kernel,
        out_shape=jax.ShapeDtypeStruct(q.shape, BF),
        scratch_shapes=[pltpu.VMEM(m.shape, F32), pltpu.VMEM(l.shape, F32), pltpu.VMEM(acc.shape, F32)],
        compiler_params=pltpu.CompilerParams(vmem_limit_bytes=MEM),
        name="image_attention",
    )(q, m, l, acc, img, kvi, qpos, qstart, ipos, iown)


def layer_kernel(tok_ref, img_ref, index_ref, o_ref):
    rows, cols = tok_ref.shape
    slots = img_ref.shape[0]
    index = index_ref[...]
    picker = (index == lax.broadcasted_iota(jnp.int32, (rows, slots), 1)).astype(F32).astype(BF)
    picked = dot_f32(picker, img_ref[...])
    o_ref[...] = jnp.where(index < slots, picked, tok_ref[...].astype(F32)).astype(BF)


def layer_input(tokens, images, index):
    rows, width = tokens.shape
    cols = width // 4
    return pl.pallas_call(
        layer_kernel,
        grid=(4,),
        in_specs=[
            pl.BlockSpec((rows, cols), lambda i: (0, i)),
            pl.BlockSpec((images.shape[0], cols), lambda i: (0, i)),
            pl.BlockSpec((rows, 1), lambda i: (0, 0)),
        ],
        out_specs=pl.BlockSpec((rows, cols), lambda i: (0, i)),
        out_shape=jax.ShapeDtypeStruct((rows, width), BF),
        compiler_params=pltpu.CompilerParams(vmem_limit_bytes=MEM),
        name="layer_input",
    )(tokens, images, index)


def output_kernel(place_ref, att_ref, in_ref, *refs):
    w_refs, (o_ref, buf_ref, sem_ref) = (refs[:-3], refs[-3:])
    step = pl.program_id(0)
    tiles, _, lanes = buf_ref.shape[1:]
    loads = piece_loads(w_refs, buf_ref, sem_ref)

    @pl.when(step == 0)
    def _():
        for load in loads:
            for copy in load:
                copy.start()

    for i, load in enumerate(loads):

        @pl.when(step == i)
        def _(load=load):
            for copy in load:
                copy.wait()

    for t in range(0, tiles, 2):
        at = slice(t * lanes, (t + 2) * lanes)
        w = jnp.concatenate([buf_ref[step, t], buf_ref[step, t + 1]], axis=1)
        o_ref[:, at] = (in_ref[:, at].astype(F32) + dot_f32(att_ref[...], w)).astype(BF)


def output_layer(place, att, layer_in, parts):
    rows, width = layer_in.shape
    tiles, depth, lanes = parts[0].shape
    column = lambda i, c: (0, c[i])
    return pl.pallas_call(
        output_kernel,
        grid_spec=pltpu.PrefetchScalarGridSpec(
            num_scalar_prefetch=1,
            grid=(8,),
            in_specs=[
                pl.BlockSpec(att.shape, lambda i, c: (0, 0)),
                pl.BlockSpec((rows, tiles * lanes), column),
            ]
            + [pl.BlockSpec(memory_space=pl.ANY)] * len(parts),
            out_specs=pl.BlockSpec((rows, tiles * lanes), column),
            scratch_shapes=[
                pltpu.VMEM((8, tiles, depth, lanes), BF),
                pltpu.SemaphoreType.DMA((len(parts),)),
            ],
        ),
        out_shape=jax.ShapeDtypeStruct((rows, width), BF),
        compiler_params=pltpu.CompilerParams(vmem_limit_bytes=MEM),
        name="output_layer",
    )(place, att, layer_in, *parts)


def swap(x, axis):
    return lax.ppermute(x, axis, [(0, 1), (1, 0)])


def after(x, *others):
    return lax.optimization_barrier((x, *others))[0]


def in_order(mine, theirs, place, dim):
    return jnp.where(place == 0, jnp.stack([mine, theirs], dim), jnp.stack([theirs, mine], dim))


def along_x(x, steps):
    place = lambda at: (at % 2) * 2 + at // 2
    return lax.ppermute(x, (XLO, XHI), [(place(at), place((at + steps) % 4)) for at in range(4)])


def neighbours_x(x):
    return along_x(x, 1), along_x(x, 3)


def around_x(x, before, behind):
    half = x.shape[0] // 2
    return [x, before, behind, along_x(before[:half], 1), along_x(behind[half:], 3)]


def both_cores(parts, *held):
    return parts + [swap(after(part, *held), CORE) for part in parts]


def copies_to(x, axes):
    count = lax.axis_size(axes)
    return lax.all_to_all(jnp.broadcast_to(x[None], (count,) + x.shape), axes, 0, 0, tiled=True)


def half_across(x, axis, core):
    size = x.shape[axis] // 2
    return swap(lax.dynamic_slice_in_dim(x, core * size, size, axis), XHI)


def both_halves(mine, axis, core):
    size = mine.shape[axis]
    buffer = jnp.zeros(mine.shape[:axis] + (2 * size,) + mine.shape[axis + 1 :], mine.dtype)
    buffer = lax.dynamic_update_slice_in_dim(buffer, mine, core * size, axis)
    return lax.dynamic_update_slice_in_dim(buffer, swap(mine, CORE), (1 - core) * size, axis)


def keys_for_later(block, x_hi, zy):
    below = lax.ppermute(block, XHI, [(0, 1)])
    count = lax.axis_size(ZY)
    receiver = jnp.arange(count, dtype=jnp.int32)
    take_below = ((x_hi == 1) & (receiver <= zy)).reshape((count,) + (1,) * block.ndim)
    outgoing = jnp.where(take_below, below[None], block[None])
    return lax.all_to_all(outgoing, ZY, 0, 0, tiled=True)


def on_device(
    patches, piece_ids, vit_gain, vit_qkv, vit_out, merge_gain, merge_up, merge_down, dest,
    tokens, image_index, doc_lengths, attn_gain, attn_qkv, attn_out,
):
    core = lax.axis_index(CORE)
    x_hi = lax.axis_index(XHI)
    zy = lax.axis_index(ZY)
    y_odd = lax.axis_index(Y) % 2
    seq_count = lax.axis_size(SEQ)
    seq_index = lax.axis_index(SEQ)
    places = seq_count // 2
    tok_rows, width = tokens.shape

    depth, sliver = attn_out.shape
    upper, lower = (attn_out[: depth // 2], attn_out[depth // 2 :])
    give = jnp.where(y_odd == 1, upper, lower)
    keep = jnp.where(y_odd == 1, lower, upper)
    got = lax.ppermute(give, Y, [(0, 1), (1, 0), (2, 3), (3, 2)])
    tile = jnp.where(
        y_odd == 1, jnp.concatenate([got, keep], axis=1), jnp.concatenate([keep, got], axis=1)
    )
    spread = copies_to(after(attn_qkv, tile), ZY)
    qkv_piece = spread.reshape(-1, attn_qkv.shape[1])
    qkv_near = neighbours_x(qkv_piece)
    qkv_parts = around_x(qkv_piece, *qkv_near)
    chip_x = x_hi * 2 + lax.axis_index(XLO)
    place = [
        (source % 2) * 4 + side * 2 + source // 2
        for side in (core, 1 - core)
        for source in [(chip_x - steps) % 4 for steps in (0, 1, 3, 2)]
    ]
    place = jnp.stack(place).astype(jnp.int32)

    up_own = merge_up.T
    up_half = half_across(up_own, 1, core)
    down_half = half_across(after(merge_down, *qkv_near), 0, core)
    up_oth = both_halves(up_half, 1, core)
    down_oth = both_halves(down_half, 0, core)

    merge_in = window_layer(after(patches, up_half), piece_ids, vit_gain, vit_qkv, vit_out, merge_gain)
    own_rows = merge_in.shape[0]
    note = jnp.broadcast_to(dest.astype(BF)[:, None], (own_rows, 128))
    rows = copies_to(after(jnp.concatenate([merge_in, note], axis=1), spread), ZY)
    rows = rows.reshape(places * own_rows, -1)
    wide = merge_in.shape[1]
    out_spread = copies_to(after(tile, rows, *qkv_near), ZY)
    out_piece = after(out_spread.reshape(-1, depth, 2 * sliver), *qkv_parts[3:])
    out_near = neighbours_x(out_piece)
    out_parts = around_x(out_piece, *out_near)
    targets = rows[:, wide].astype(jnp.int32)

    def hidden(weights):
        total = dot_f32(weights, rows[:, :wide], 1, 1)
        return jax.nn.gelu(total, approximate=False).astype(BF)

    mine, theirs = (hidden(up_own), hidden(up_oth))
    pair = after(in_order(mine, theirs, x_hi, 0), out_spread)
    gathered = copies_to(pair, ZY)
    qkv_all = both_cores(qkv_parts, pair)

    hidden_0, hidden_1 = (gathered[:, i].reshape(-1, places * own_rows) for i in range(2))
    middle = hidden_0.shape[0]

    def columns(weights):
        return (
            dot_f32(hidden_0, weights[:middle], 0, 0) + dot_f32(hidden_1, weights[middle:], 0, 0)
        ).astype(BF)

    mine, theirs = (columns(merge_down), columns(down_oth))
    merged = jnp.concatenate(
        [jnp.where(x_hi == 0, mine, theirs), jnp.where(x_hi == 0, theirs, mine)], axis=1
    )

    receivers = jnp.arange(seq_count, dtype=jnp.int32)
    row_home = jnp.arange(places * own_rows, dtype=jnp.int32) // own_rows
    homes = jnp.arange(places, dtype=jnp.int32)
    select = (targets[None, None, :] == receivers[:, None, None]) & (
        row_home[None, None, :] == homes[None, :, None]
    )
    outgoing = dot_f32(select.astype(BF).reshape(seq_count * places, -1), merged).astype(BF)
    proj_text = project(place, after(tokens, outgoing), attn_gain, qkv_all)
    query_width = depth
    index_row = jnp.broadcast_to(image_index.astype(BF)[None, :], (16, tok_rows))
    block = jnp.concatenate([proj_text[:, query_width:], index_row], axis=0)
    block = after(block, *out_near)
    kv_text = keys_for_later(block, x_hi, zy)
    arrived = lax.all_to_all(
        outgoing.reshape(seq_count, places, -1), SEQ, split_axis=0, concat_axis=0, tiled=True
    )
    arrived = arrived.reshape(2, places, places, 2, -1)
    images = arrived.transpose(0, 2, 3, 1, 4).reshape(seq_count, width)

    proj_img = project(place, images, attn_gain, qkv_all)
    kv_img = keys_for_later(after(proj_img[:, query_width:], *out_parts[3:]), x_hi, zy)

    positions = seq_index * tok_rows + jnp.arange(tok_rows, dtype=jnp.int32)
    lengths = doc_lengths[0]
    order_of = jnp.arange(lengths.shape[0], dtype=jnp.int32)
    starts = jnp.sum(jnp.where(order_of[None, :] < order_of[:, None], lengths[None, :], 0), axis=1)
    doc_start = jnp.max(jnp.where(starts[None, :] <= positions[:, None], starts[None, :], 0), axis=1)
    slot_ids = jnp.arange(seq_count, dtype=jnp.int32)
    within = jnp.arange(tok_rows, dtype=jnp.int32)
    home = jnp.where(x_hi == 0, homes, jnp.where(homes >= zy, homes, homes + places))
    useful = (x_hi == 1) | (homes < zy)
    indexes = kv_text[:, tok_rows, :].astype(jnp.int32)
    kpos = jnp.where(
        (indexes == seq_count) & useful[:, None], home[:, None] * tok_rows + within[None, :], FAR
    )
    ownpos = jnp.where(image_index == seq_count, positions, FAR)
    hits = indexes[:, None, :] == slot_ids[None, :, None]
    ipos = jnp.min(
        jnp.where(hits & useful[:, None, None], (home[:, None] * tok_rows + within[None, :])[:, None, :], FAR),
        axis=-1,
    )
    iown = jnp.min(
        jnp.where(image_index[None, :] == slot_ids[:, None], positions[None, :], FAR), axis=-1
    )

    out_all = both_cores(out_parts, proj_text)
    index_col = image_index.reshape(tok_rows, 1)
    qpos, qstart = (positions.reshape(tok_rows, 1), doc_start.reshape(tok_rows, 1))
    query, high, total, mixed = text_attention(
        proj_text, proj_img, kv_text, index_col, qpos, qstart,
        kpos.reshape(places // 2, 1, 2 * tok_rows), ownpos.reshape(1, tok_rows),
    )
    layer_in = layer_input(tokens, images, after(index_col, proj_img))
    attended = image_attention(
        query, high, total, mixed, proj_img, kv_img.reshape(-1, kv_img.shape[2]),
        qpos, qstart, ipos.reshape(1, -1), iown.reshape(1, -1),
    )
    return output_layer(place, attended, layer_in, out_all)


def solution(mesh):
    torus = Mesh(mesh.devices.reshape(2, 2, 2, 4, 4), GRP_SEQ)
    return jax.shard_map(
        on_device,
        mesh=torus,
        in_specs=(
            P(GRP_SEQ, None),
            P(GRP_SEQ, None),
            P(),
            P(),
            P(),
            P(),
            P(None, SEQ),
            P(None, SEQ),
            P(GRP_SEQ),
            P(GRP_SEQ, None),
            P(GRP_SEQ),
            P(GRP, None),
            P(),
            P(GRP_SEQ, None),
            P(None, GRP_SEQ),
        ),
        out_specs=P(GRP_SEQ, None),
        check_vma=False,
    )
```

```python
import jax
import jax.numpy as jnp
from jax import lax
from jax.experimental import pallas as pl
from jax.experimental.pallas import tpu as pltpu
from jax.sharding import Mesh
from jax.sharding import PartitionSpec as P

VHEADS = 16
XLO, CORE, XHI, Z, Y = ("grp_0", "grp_1", "seq_0", "seq_1", "seq_2")
SEQ = (XHI, Z, Y)
ZY = (Z, Y)
GRP_SEQ = (XLO, CORE, XHI, Z, Y)
GRP = (XLO, CORE)
EPSILON = 1e-06
NEG = -1e30
FAR = 1 << 30
BF = jnp.bfloat16
F32 = jnp.float32
MEM = 56 * 1024 * 1024


def dot_f32(a, b, ca=1, cb=0):
    return lax.dot_general(a, b, (((ca,), (cb,)), ((), ())), preferred_element_type=F32)


def window_kernel(x_ref, prow_ref, pcol_ref, gain_ref, w_ref, wo_ref, mgain_ref, o_ref, n_ref, p_ref):
    step = pl.program_id(0)
    rows, feats = x_ref.shape
    head = feats // VHEADS

    @pl.when(step == 0)
    def _():
        x = x_ref[...].astype(F32)
        mean = jnp.mean(x * x, axis=-1, keepdims=True)
        n_ref[...] = (x * lax.rsqrt(mean + EPSILON) * gain_ref[...]).astype(BF)

    for part in range(3):

        @pl.when(step == part)
        def _(part=part):
            p_ref[part] = dot_f32(n_ref[...], w_ref[...]).astype(BF)

    @pl.when(step == 2)
    def _():
        q, k, v = (p_ref[0], p_ref[1], p_ref[2])
        lane = lax.broadcasted_iota(jnp.int32, (rows, feats), 1)
        same = pcol_ref[...] == prow_ref[...]
        mixed = jnp.zeros((rows, feats), F32)
        for h in range(VHEADS):
            mine = (lane >= h * head) & (lane < (h + 1) * head)
            s = dot_f32(jnp.where(mine, q, jnp.zeros_like(q)), k, 1, 1) * head ** (-0.5)
            s = jnp.where(same, s, NEG)
            w = jnp.exp(s - jnp.max(s, axis=-1, keepdims=True))
            total = jnp.sum(w, axis=-1, keepdims=True)
            mixed = jnp.where(mine, dot_f32(w.astype(BF), v) / total, mixed)
        resid = x_ref[...].astype(F32) + dot_f32(mixed.astype(BF), wo_ref[...])
        mean = jnp.mean(resid * resid, axis=-1, keepdims=True)
        merged = (resid * lax.rsqrt(mean + EPSILON) * mgain_ref[...]).astype(BF)
        r_out = lax.broadcasted_iota(jnp.int32, (rows // 4, rows), 0)
        r_in = lax.broadcasted_iota(jnp.int32, (rows // 4, rows), 1)
        for j in range(4):
            pick = jnp.where(r_in == 4 * r_out + j, 1.0, 0.0).astype(BF)
            o_ref[:, j * feats : (j + 1) * feats] = dot_f32(pick, merged).astype(BF)


def window_layer(patches, piece_ids, vit_gain, vit_qkv, vit_out, merge_gain):
    rows, feats = patches.shape
    whole = lambda *shape: pl.BlockSpec(shape, lambda i: (0,) * len(shape))
    return pl.pallas_call(
        window_kernel,
        grid=(3,),
        in_specs=[
            whole(rows, feats),
            whole(1, rows),
            whole(rows, 1),
            whole(1, feats),
            pl.BlockSpec((feats, feats), lambda i: (0, i)),
            whole(feats, feats),
            whole(1, feats),
        ],
        out_specs=whole(rows // 4, 4 * feats),
        out_shape=jax.ShapeDtypeStruct((rows // 4, 4 * feats), BF),
        scratch_shapes=[pltpu.VMEM((rows, feats), BF), pltpu.VMEM((3, rows, feats), BF)],
        compiler_params=pltpu.CompilerParams(vmem_limit_bytes=MEM),
        name="window_layer",
    )(
        patches,
        piece_ids.reshape(1, rows),
        piece_ids.reshape(rows, 1),
        vit_gain.reshape(1, feats),
        vit_qkv,
        vit_out,
        merge_gain.reshape(1, feats),
    )


def piece_loads(refs, buf_ref, sem_ref):
    half = buf_ref.shape[1] // 2
    loads = []
    for side in range(2):
        own = refs[side * 5 : side * 5 + 5]
        for k in range(4):
            slot = side * 4 + k
            if k < 3:
                spots = [(own[k], buf_ref.at[slot])]
            else:
                spots = [(own[3 + i], buf_ref.at[slot, pl.ds(i * half, half)]) for i in range(2)]
            loads.append(
                [pltpu.make_async_copy(w, spot, sem_ref.at[side * 5 + k + i]) for i, (w, spot) in enumerate(spots)]
            )
    return loads


def project_kernel(place_ref, x_ref, gain_ref, *refs):
    w_refs, (o_ref, buf_ref, sem_ref) = (refs[:-3], refs[-3:])
    rows, width = x_ref.shape
    depth = buf_ref.shape[1]
    loads = piece_loads(w_refs, buf_ref, sem_ref)
    for load in loads:
        for copy in load:
            copy.start()
    total = jnp.zeros((rows, 1), F32)
    for c in range(0, width, depth):
        x = x_ref[:, c : c + depth].astype(F32)
        total = total + jnp.sum(x * x, axis=-1, keepdims=True)
    scale = lax.rsqrt(total / width + EPSILON)
    acc = jnp.zeros(o_ref.shape, F32)
    for i, load in enumerate(loads):
        start = pl.multiple_of(place_ref[i] * depth, depth)
        x = x_ref[:, pl.ds(start, depth)].astype(F32)
        n = (x * scale * gain_ref[:, pl.ds(start, depth)]).astype(BF)
        for copy in load:
            copy.wait()
        acc = acc + dot_f32(n, buf_ref[i])
    o_ref[...] = acc.astype(BF)


def project(place, x, gain, parts):
    rows, width = x.shape
    depth, cols = parts[0].shape
    return pl.pallas_call(
        project_kernel,
        grid_spec=pltpu.PrefetchScalarGridSpec(
            num_scalar_prefetch=1,
            grid=(1,),
            in_specs=[
                pl.BlockSpec((rows, width), lambda i, c: (0, 0)),
                pl.BlockSpec((1, width), lambda i, c: (0, 0)),
            ]
            + [pl.BlockSpec(memory_space=pl.ANY)] * len(parts),
            out_specs=pl.BlockSpec((rows, cols), lambda i, c: (0, 0)),
            scratch_shapes=[
                pltpu.VMEM((8, depth, cols), BF),
                pltpu.SemaphoreType.DMA((len(parts),)),
            ],
        ),
        out_shape=jax.ShapeDtypeStruct((rows, cols), BF),
        compiler_params=pltpu.CompilerParams(vmem_limit_bytes=MEM),
        name="project",
    )(place, x, gain.reshape(1, width), *parts)


def fold_keys(query, keys, values, allowed, h, scale, m_ref, l_ref, acc_ref):
    s = jnp.where(allowed, dot_f32(query, keys, 1, 1) * scale, NEG)
    old = m_ref[h]
    new = jnp.maximum(old, jnp.max(s, axis=-1, keepdims=True))
    shrink = jnp.exp(old - new)
    w = jnp.exp(s - new)
    l_ref[h] = l_ref[h] * shrink + jnp.sum(w, axis=-1, keepdims=True)
    acc_ref[h] = acc_ref[h] * shrink + dot_f32(w.astype(BF), values)
    m_ref[h] = new


def text_kernel(
    own_ref, img_ref, kv_ref, index_ref, qpos_ref, qstart_ref, kpos_ref, ownpos_ref,
    q_ref, m_ref, l_ref, acc_ref,
):
    rows = own_ref.shape[0]
    slots = img_ref.shape[0]
    head = kv_ref.shape[2] // 2
    width = q_ref.shape[1]
    heads = width // head
    blocks = kv_ref.shape[0]
    m_ref[...] = jnp.full_like(m_ref, NEG)
    l_ref[...] = jnp.zeros_like(l_ref)
    acc_ref[...] = jnp.zeros_like(acc_ref)
    index = index_ref[...]
    picker = (index == lax.broadcasted_iota(jnp.int32, (rows, slots), 1)).astype(F32).astype(BF)
    q_ref[...] = jnp.where(
        index < slots, dot_f32(picker, img_ref[:, :width]), own_ref[:, :width].astype(F32)
    ).astype(BF)
    qpos, qstart = (qpos_ref[...], qstart_ref[...])

    def fold(keys, values, kpos):
        allowed = (kpos >= qstart) & (kpos <= qpos)
        for h in range(heads):
            query = q_ref[:, h * head : (h + 1) * head]
            fold_keys(query, keys, values, allowed, h, head ** (-0.5), m_ref, l_ref, acc_ref)

    fold(own_ref[:, width : width + head], own_ref[:, width + head :], ownpos_ref[...])

    def step(i, carry):
        pair = kv_ref[pl.ds(2 * i, 2), :rows, :].reshape(2 * rows, 2 * head)
        fold(pair[:, :head], pair[:, head:], kpos_ref[i])
        return carry

    lax.fori_loop(0, blocks // 2, step, 0)


def text_attention(own, img, kv, index, qpos, qstart, kpos, ownpos):
    rows = own.shape[0]
    head = kv.shape[2] // 2
    heads = (own.shape[1] - 2 * head) // head
    return pl.pallas_call(
        text_kernel,
        out_shape=(
            jax.ShapeDtypeStruct((rows, heads * head), BF),
            jax.ShapeDtypeStruct((heads, rows, 1), F32),
            jax.ShapeDtypeStruct((heads, rows, 1), F32),
            jax.ShapeDtypeStruct((heads, rows, head), F32),
        ),
        compiler_params=pltpu.CompilerParams(vmem_limit_bytes=MEM),
        name="text_attention",
    )(own, img, kv, index, qpos, qstart, kpos, ownpos)


def image_kernel(
    q_ref, m_in, l_in, acc_in, img_ref, kvi_ref, qpos_ref, qstart_ref, ipos_ref, iown_ref,
    o_ref, m_ref, l_ref, acc_ref,
):
    head = acc_in.shape[2]
    heads = acc_in.shape[0]
    width = heads * head
    m_ref[...] = m_in[...]
    l_ref[...] = l_in[...]
    acc_ref[...] = acc_in[...]
    qpos, qstart = (qpos_ref[...], qstart_ref[...])
    for keys, values, kpos in (
        (kvi_ref[:, :head], kvi_ref[:, head:], ipos_ref[...]),
        (img_ref[:, width : width + head], img_ref[:, width + head :], iown_ref[...]),
    ):
        allowed = (kpos >= qstart) & (kpos <= qpos)
        for h in range(heads):
            query = q_ref[:, h * head : (h + 1) * head]
            fold_keys(query, keys, values, allowed, h, head ** (-0.5), m_ref, l_ref, acc_ref)
    for h in range(heads):
        o_ref[:, h * head : (h + 1) * head] = (acc_ref[h] / l_ref[h]).astype(BF)


def image_attention(q, m, l, acc, img, kvi, qpos, qstart, ipos, iown):
    return pl.pallas_call(
        image_kernel,
        out_shape=jax.ShapeDtypeStruct(q.shape, BF),
        scratch_shapes=[pltpu.VMEM(m.shape, F32), pltpu.VMEM(l.shape, F32), pltpu.VMEM(acc.shape, F32)],
        compiler_params=pltpu.CompilerParams(vmem_limit_bytes=MEM),
        name="image_attention",
    )(q, m, l, acc, img, kvi, qpos, qstart, ipos, iown)


def layer_kernel(tok_ref, img_ref, index_ref, o_ref):
    rows, cols = tok_ref.shape
    slots = img_ref.shape[0]
    index = index_ref[...]
    picker = (index == lax.broadcasted_iota(jnp.int32, (rows, slots), 1)).astype(F32).astype(BF)
    picked = dot_f32(picker, img_ref[...])
    o_ref[...] = jnp.where(index < slots, picked, tok_ref[...].astype(F32)).astype(BF)


def layer_input(tokens, images, index):
    rows, width = tokens.shape
    cols = width // 4
    return pl.pallas_call(
        layer_kernel,
        grid=(4,),
        in_specs=[
            pl.BlockSpec((rows, cols), lambda i: (0, i)),
            pl.BlockSpec((images.shape[0], cols), lambda i: (0, i)),
            pl.BlockSpec((rows, 1), lambda i: (0, 0)),
        ],
        out_specs=pl.BlockSpec((rows, cols), lambda i: (0, i)),
        out_shape=jax.ShapeDtypeStruct((rows, width), BF),
        compiler_params=pltpu.CompilerParams(vmem_limit_bytes=MEM),
        name="layer_input",
    )(tokens, images, index)


def output_kernel(place_ref, att_ref, in_ref, *refs):
    w_refs, (o_ref, buf_ref, sem_ref) = (refs[:-3], refs[-3:])
    step = pl.program_id(0)
    tiles, _, lanes = buf_ref.shape[1:]
    loads = piece_loads(w_refs, buf_ref, sem_ref)

    @pl.when(step == 0)
    def _():
        for load in loads:
            for copy in load:
                copy.start()

    for i, load in enumerate(loads):

        @pl.when(step == i)
        def _(load=load):
            for copy in load:
                copy.wait()

    for t in range(0, tiles, 2):
        at = slice(t * lanes, (t + 2) * lanes)
        w = jnp.concatenate([buf_ref[step, t], buf_ref[step, t + 1]], axis=1)
        o_ref[:, at] = (in_ref[:, at].astype(F32) + dot_f32(att_ref[...], w)).astype(BF)


def output_layer(place, att, layer_in, parts):
    rows, width = layer_in.shape
    tiles, depth, lanes = parts[0].shape
    column = lambda i, c: (0, c[i])
    return pl.pallas_call(
        output_kernel,
        grid_spec=pltpu.PrefetchScalarGridSpec(
            num_scalar_prefetch=1,
            grid=(8,),
            in_specs=[
                pl.BlockSpec(att.shape, lambda i, c: (0, 0)),
                pl.BlockSpec((rows, tiles * lanes), column),
            ]
            + [pl.BlockSpec(memory_space=pl.ANY)] * len(parts),
            out_specs=pl.BlockSpec((rows, tiles * lanes), column),
            scratch_shapes=[
                pltpu.VMEM((8, tiles, depth, lanes), BF),
                pltpu.SemaphoreType.DMA((len(parts),)),
            ],
        ),
        out_shape=jax.ShapeDtypeStruct((rows, width), BF),
        compiler_params=pltpu.CompilerParams(vmem_limit_bytes=MEM),
        name="output_layer",
    )(place, att, layer_in, *parts)


def swap(x, axis):
    return lax.ppermute(x, axis, [(0, 1), (1, 0)])


def after(x, *others):
    return lax.optimization_barrier((x, *others))[0]


def in_order(mine, theirs, place, dim):
    return jnp.where(place == 0, jnp.stack([mine, theirs], dim), jnp.stack([theirs, mine], dim))


def along_x(x, steps):
    place = lambda at: (at % 2) * 2 + at // 2
    return lax.ppermute(x, (XLO, XHI), [(place(at), place((at + steps) % 4)) for at in range(4)])


def neighbours_x(x):
    return along_x(x, 1), along_x(x, 3)


def around_x(x, before, behind):
    half = x.shape[0] // 2
    return [x, before, behind, along_x(before[:half], 1), along_x(behind[half:], 3)]


def both_cores(parts, *held):
    return parts + [swap(after(part, *held), CORE) for part in parts]


def copies_to(x, axes):
    count = lax.axis_size(axes)
    return lax.all_to_all(jnp.broadcast_to(x[None], (count,) + x.shape), axes, 0, 0, tiled=True)


def half_across(x, axis, core):
    size = x.shape[axis] // 2
    return swap(lax.dynamic_slice_in_dim(x, core * size, size, axis), XHI)


def both_halves(mine, axis, core):
    size = mine.shape[axis]
    buffer = jnp.zeros(mine.shape[:axis] + (2 * size,) + mine.shape[axis + 1 :], mine.dtype)
    buffer = lax.dynamic_update_slice_in_dim(buffer, mine, core * size, axis)
    return lax.dynamic_update_slice_in_dim(buffer, swap(mine, CORE), (1 - core) * size, axis)


def keys_for_later(block, x_hi, zy):
    below = lax.ppermute(block, XHI, [(0, 1)])
    count = lax.axis_size(ZY)
    receiver = jnp.arange(count, dtype=jnp.int32)
    take_below = ((x_hi == 1) & (receiver <= zy)).reshape((count,) + (1,) * block.ndim)
    outgoing = jnp.where(take_below, below[None], block[None])
    return lax.all_to_all(outgoing, ZY, 0, 0, tiled=True)


def on_device(
    patches, piece_ids, vit_gain, vit_qkv, vit_out, merge_gain, merge_up, merge_down, dest,
    tokens, image_index, doc_lengths, attn_gain, attn_qkv, attn_out,
):
    core = lax.axis_index(CORE)
    x_hi = lax.axis_index(XHI)
    zy = lax.axis_index(ZY)
    y_odd = lax.axis_index(Y) % 2
    seq_count = lax.axis_size(SEQ)
    seq_index = lax.axis_index(SEQ)
    places = seq_count // 2
    tok_rows, width = tokens.shape

    depth, sliver = attn_out.shape
    spread = copies_to(attn_qkv, ZY)
    qkv_piece = spread.reshape(-1, attn_qkv.shape[1])
    qkv_near = neighbours_x(qkv_piece)
    qkv_parts = around_x(qkv_piece, *qkv_near)
    upper, lower = (attn_out[: depth // 2], attn_out[depth // 2 :])
    give = jnp.where(y_odd == 1, upper, lower)
    keep = jnp.where(y_odd == 1, lower, upper)
    got = lax.ppermute(after(give, spread), Y, [(0, 1), (1, 0), (2, 3), (3, 2)])
    tile = jnp.where(
        y_odd == 1, jnp.concatenate([got, keep], axis=1), jnp.concatenate([keep, got], axis=1)
    )
    chip_x = x_hi * 2 + lax.axis_index(XLO)
    place = [
        (source % 2) * 4 + side * 2 + source // 2
        for side in (core, 1 - core)
        for source in [(chip_x - steps) % 4 for steps in (0, 1, 3, 2)]
    ]
    place = jnp.stack(place).astype(jnp.int32)

    up_own = merge_up.T
    up_half = half_across(up_own, 1, core)
    down_half = half_across(after(merge_down, *qkv_near), 0, core)
    up_oth = both_halves(up_half, 1, core)
    down_oth = both_halves(down_half, 0, core)

    merge_in = window_layer(after(patches, up_half), piece_ids, vit_gain, vit_qkv, vit_out, merge_gain)
    own_rows = merge_in.shape[0]
    note = jnp.broadcast_to(dest.astype(BF)[:, None], (own_rows, 128))
    rows = copies_to(after(jnp.concatenate([merge_in, note], axis=1), spread), ZY)
    rows = rows.reshape(places * own_rows, -1)
    wide = merge_in.shape[1]
    out_spread = copies_to(after(tile, rows, *qkv_near), ZY)
    out_piece = after(out_spread.reshape(-1, depth, 2 * sliver), *qkv_parts[3:])
    out_near = neighbours_x(out_piece)
    out_parts = around_x(out_piece, *out_near)
    targets = rows[:, wide].astype(jnp.int32)

    def hidden(weights):
        total = dot_f32(weights, rows[:, :wide], 1, 1)
        return jax.nn.gelu(total, approximate=False).astype(BF)

    mine, theirs = (hidden(up_own), hidden(up_oth))
    pair = after(in_order(mine, theirs, x_hi, 0), out_spread)
    gathered = copies_to(pair, ZY)
    qkv_all = both_cores(qkv_parts, pair)

    hidden_0, hidden_1 = (gathered[:, i].reshape(-1, places * own_rows) for i in range(2))
    middle = hidden_0.shape[0]

    def columns(weights):
        return (
            dot_f32(hidden_0, weights[:middle], 0, 0) + dot_f32(hidden_1, weights[middle:], 0, 0)
        ).astype(BF)

    mine, theirs = (columns(merge_down), columns(down_oth))
    merged = jnp.concatenate(
        [jnp.where(x_hi == 0, mine, theirs), jnp.where(x_hi == 0, theirs, mine)], axis=1
    )

    receivers = jnp.arange(seq_count, dtype=jnp.int32)
    row_home = jnp.arange(places * own_rows, dtype=jnp.int32) // own_rows
    homes = jnp.arange(places, dtype=jnp.int32)
    select = (targets[None, None, :] == receivers[:, None, None]) & (
        row_home[None, None, :] == homes[None, :, None]
    )
    outgoing = dot_f32(select.astype(BF).reshape(seq_count * places, -1), merged).astype(BF)
    proj_text = project(place, after(tokens, outgoing), attn_gain, qkv_all)
    query_width = depth
    index_row = jnp.broadcast_to(image_index.astype(BF)[None, :], (16, tok_rows))
    block = jnp.concatenate([proj_text[:, query_width:], index_row], axis=0)
    block = after(block, *out_near)
    kv_text = keys_for_later(block, x_hi, zy)
    arrived = lax.all_to_all(
        outgoing.reshape(seq_count, places, -1), SEQ, split_axis=0, concat_axis=0, tiled=True
    )
    arrived = arrived.reshape(2, places, places, 2, -1)
    images = arrived.transpose(0, 2, 3, 1, 4).reshape(seq_count, width)

    proj_img = project(place, images, attn_gain, qkv_all)
    kv_img = keys_for_later(after(proj_img[:, query_width:], *out_parts[3:]), x_hi, zy)

    positions = seq_index * tok_rows + jnp.arange(tok_rows, dtype=jnp.int32)
    lengths = doc_lengths[0]
    order_of = jnp.arange(lengths.shape[0], dtype=jnp.int32)
    starts = jnp.sum(jnp.where(order_of[None, :] < order_of[:, None], lengths[None, :], 0), axis=1)
    doc_start = jnp.max(jnp.where(starts[None, :] <= positions[:, None], starts[None, :], 0), axis=1)
    slot_ids = jnp.arange(seq_count, dtype=jnp.int32)
    within = jnp.arange(tok_rows, dtype=jnp.int32)
    home = jnp.where(x_hi == 0, homes, jnp.where(homes >= zy, homes, homes + places))
    useful = (x_hi == 1) | (homes < zy)
    indexes = kv_text[:, tok_rows, :].astype(jnp.int32)
    kpos = jnp.where(
        (indexes == seq_count) & useful[:, None], home[:, None] * tok_rows + within[None, :], FAR
    )
    ownpos = jnp.where(image_index == seq_count, positions, FAR)
    hits = indexes[:, None, :] == slot_ids[None, :, None]
    ipos = jnp.min(
        jnp.where(hits & useful[:, None, None], (home[:, None] * tok_rows + within[None, :])[:, None, :], FAR),
        axis=-1,
    )
    iown = jnp.min(
        jnp.where(image_index[None, :] == slot_ids[:, None], positions[None, :], FAR), axis=-1
    )

    out_all = both_cores(out_parts, proj_text)
    index_col = image_index.reshape(tok_rows, 1)
    qpos, qstart = (positions.reshape(tok_rows, 1), doc_start.reshape(tok_rows, 1))
    query, high, total, mixed = text_attention(
        proj_text, proj_img, kv_text, index_col, qpos, qstart,
        kpos.reshape(places // 2, 1, 2 * tok_rows), ownpos.reshape(1, tok_rows),
    )
    layer_in = layer_input(tokens, images, after(index_col, proj_img))
    attended = image_attention(
        query, high, total, mixed, proj_img, kv_img.reshape(-1, kv_img.shape[2]),
        qpos, qstart, ipos.reshape(1, -1), iown.reshape(1, -1),
    )
    return output_layer(place, attended, layer_in, out_all)


def solution(mesh):
    torus = Mesh(mesh.devices.reshape(2, 2, 2, 4, 4), GRP_SEQ)
    return jax.shard_map(
        on_device,
        mesh=torus,
        in_specs=(
            P(GRP_SEQ, None),
            P(GRP_SEQ, None),
            P(),
            P(),
            P(),
            P(),
            P(None, SEQ),
            P(None, SEQ),
            P(GRP_SEQ),
            P(GRP_SEQ, None),
            P(GRP_SEQ),
            P(GRP, None),
            P(),
            P(GRP_SEQ, None),
            P(None, GRP_SEQ),
        ),
        out_specs=P(GRP_SEQ, None),
        check_vma=False,
    )
```
